32 devices in a mesh: grp: 2 (over x), ex: 8 (over z, y), lay: 2 (over core).
Axes of the slice: x: 2, y: 2, z: 4, core: 2. Of those that a mesh axis runs over, the one named last changes fastest.
Arguments:
- queries: bfloat16 [512, 2, 4096], P('ex', 'lay'), may hold values from -4 to 4
- basis_s: float32 [2, 64, 64], P('lay'), may hold values from -1 to 1, as said below
- basis_a: float32 [2, 64, 64], P('lay'), may hold values from -1 to 1, as said below
- eigvals: float32 [2, 64, 64], P('lay'), may hold values from 0.004 to 20, as said below
- train_grads: bfloat16 [16384, 2, 4096], P(('grp', 'ex'), 'lay'), parts along dimension 0, may hold values from -0.0625 to 0.0625
- example_ids: int32 [16, 1024], P(('grp', 'ex')), parts along dimension 0, may hold values from 0 to 1023, each once within a row
Outputs:
- scores: float32 [512, 16384], P(None, ('grp', 'ex', 'lay')), parts along dimension 1
The draws below stay inside these ranges and needn't reach their ends.
There are 2 independent parts, one for each index of `grp`. The reference program is written for one: setup_inputs(seed, part) draws one part's arguments, and reference() takes and returns one part's arrays. A program takes and returns all parts, laid end to end along the dimension named above; an argument that names none is the same for every part. Nothing has to cross between parts.
Inputs may be any that keep to these rules, and one draw needn't show every extreme that they name: `basis_s`: each layer's basis has orthonormal columns. `basis_a`: each layer's basis has orthonormal columns. `eigvals`: positive.
All inputs are finite; a program needn't handle non-finite values.
Results may differ from the reference program's by a relative error of at most 0.0029.
Values may be sent and summed in bfloat16 or wider, within the bound.
A program may use at most 64 MiB of HBM per device.

```python
import math
import jax
import jax.numpy as jnp
from jax import lax

R = 64
F = 4096
LAYERS = 2
Q = 512
EXD = 1024
EXAMPLES = 8192
N_EX = 8


def cosine_basis(key):

    def one_layer(layer_key):
        key_rows, key_cols, key_signs = jax.random.split(layer_key, 3)
        row_perm = jax.random.permutation(key_rows, R).astype(jnp.float32)
        col_perm = jax.random.permutation(key_cols, R).astype(jnp.float32)
        signs = (jax.random.randint(key_signs, (R,), 0, 2) * 2 - 1).astype(jnp.float32)
        angles = math.pi * (row_perm[:, None] + 0.5) * col_perm[None, :] / R
        norms = jnp.where(col_perm[None, :] == 0.0, math.sqrt(1.0 / R), math.sqrt(2.0 / R))
        return jnp.cos(angles) * norms * signs[None, :]
    return jax.vmap(one_layer)(jax.random.split(key, LAYERS))


def draw_basis_s(key, part):
    return cosine_basis(jax.random.fold_in(key, 11))


def draw_basis_a(key, part):
    return cosine_basis(jax.random.fold_in(key, 23))


def draw_eigvals(key, part):
    own_key = jax.random.fold_in(key, 37)
    key_one = jax.random.fold_in(own_key, 0)
    return jnp.exp(jax.random.uniform(key_one, (LAYERS, R, R), jnp.float32, math.log(0.05), math.log(20.0)))


def block_levels(key, shape, cuts, low, high):
    level, own = 1.0, jax.random.fold_in(key, 6)
    for dim, shards_of in cuts:
        steps = jnp.exp(jax.random.uniform(jax.random.fold_in(own, dim), (shards_of,), jnp.float32, low / len(cuts), high / len(cuts)))
        level = level * jnp.repeat(steps, shape[dim] // shards_of).reshape([-1 if axis == dim else 1 for axis in range(len(shape))])
    return level


def bell_draw(key, shape, deviation, most, cuts=(), kind=jnp.bfloat16):
    gain = block_levels(key, shape, cuts, -0.22, 0.18) if cuts else 1.0
    result = jax.random.normal(key, shape, jnp.float32) * deviation * gain
    return jnp.minimum(jnp.maximum(result, -most), most).astype(kind)


def setup_inputs(seed: int = 0, part: int = 0) -> dict:
    keys = jax.random.split(jax.random.key(seed), 7)
    part_keys = jax.random.split(jax.random.fold_in(keys[6], part), 7)
    queries = bell_draw(keys[0], (Q, LAYERS, F), 0.5, 4.0, ((0, 8), (1, 2)))
    basis_s = draw_basis_s(jax.random.fold_in(keys[6], 71), part)
    basis_a = draw_basis_a(jax.random.fold_in(keys[6], 71), part)
    eigvals = draw_eigvals(jax.random.fold_in(keys[6], 71), part)
    train_grads = bell_draw(part_keys[4], (EXAMPLES, LAYERS, F), (LAYERS * F) ** -0.5, 0.0625, ((0, 8), (1, 2)))
    example_ids = jax.vmap(lambda own: jax.random.permutation(own, EXD))(jax.random.split(part_keys[5], N_EX)).reshape((N_EX, EXD)).astype(jnp.int32)
    return {"queries": queries, "basis_s": basis_s, "basis_a": basis_a, "eigvals": eigvals, "train_grads": train_grads, "example_ids": example_ids}


damp_ratio = 0.1


def precondition(grads, basis_s, basis_a, eigvals):
    number_rows = grads.shape[0]
    layer_count = grads.shape[1]
    rank = basis_s.shape[-1]
    highest = lax.Precision.HIGHEST
    expanded = grads.astype(jnp.float32).reshape(number_rows, layer_count, rank, rank)
    half_turn = jnp.einsum('nlik,lkm->nlim', expanded, basis_a, precision=highest)
    rotated = jnp.einsum('lij,nlim->nljm', basis_s, half_turn, precision=highest)
    damping = damp_ratio * jnp.mean(eigvals, axis=(1, 2), keepdims=True)
    scaled = rotated / (eigvals + damping)[None]
    turned_back = jnp.einsum('nljm,lpm->nljp', scaled, basis_a, precision=highest)
    restored = jnp.einsum('lij,nljp->nlip', basis_s, turned_back, precision=highest)
    return restored.reshape(number_rows, layer_count, rank * rank).astype(jnp.bfloat16)


def reference(queries, basis_s, basis_a, eigvals, train_grads, example_ids):
    conditioned = precondition(queries, basis_s, basis_a, eigvals)
    summed = jnp.zeros((Q, EXAMPLES), jnp.float32)
    for layer in range(LAYERS):
        summed = summed + jnp.dot(conditioned[:, layer], train_grads[:, layer].T, preferred_element_type=jnp.float32)
    block_rows = (jnp.arange(N_EX, dtype=jnp.int32)[:, None] * EXD + example_ids.astype(jnp.int32)).reshape(-1)
    return jnp.take(summed, block_rows, axis=1)
```

```python
import functools

import jax
import jax.numpy as jnp
from jax import lax
from jax.experimental import pallas as pl
from jax.experimental.pallas import tpu as pltpu
from jax.sharding import PartitionSpec as P

damp_ratio = 0.1
chunks = 8
loads = 4
window = 256
MESH = pl.DeviceIdType.MESH


def precondition(grads, basis_s, basis_a, eigvals):
    number_rows = grads.shape[0]
    layer_count = grads.shape[1]
    rank = basis_s.shape[-1]
    high = lax.Precision.HIGH
    expanded = grads.astype(jnp.float32).reshape(number_rows, layer_count, rank, rank)
    half_turn = jnp.einsum("nlik,lkm->nlim", expanded, basis_a, precision=high)
    rotated = jnp.einsum("lij,nlim->nljm", basis_s, half_turn, precision=high)
    damping = damp_ratio * jnp.mean(eigvals, axis=(1, 2), keepdims=True)
    scaled = rotated / (eigvals + damping)[None]
    turned_back = jnp.einsum("nljm,lpm->nljp", scaled, basis_a, precision=high)
    restored = jnp.einsum("lij,nljp->nlip", basis_s, turned_back, precision=high)
    return restored.reshape(number_rows, layer_count, rank * rank).astype(jnp.bfloat16)


def score_kernel(
    line, own_ref, ids_ref, train_ref, out_ref,
    stored, hot, perm, held, acc, arrived, total,
    load_sem, own_sem, z_recv, y_recv, x_recv, zr_send, zl_send, y_send, x_send, c_recv, c_send, out_sem,
):
    grp = lax.axis_index("grp")
    ex = lax.axis_index("ex")
    core = lax.axis_index("lay")
    zz = ex // 2
    w = ex % 2
    side = grp % 2
    rows = own_ref.shape[1]
    examples = train_ref.shape[0]
    chunk = own_ref.shape[2]
    half = examples // 2
    wide = train_ref.shape[1] // loads
    per_load = chunks // loads
    right = {"ex": lax.rem(ex + 2, 2 * line)}
    left = {"ex": lax.rem(ex + 2 * line - 2, 2 * line)}
    across_y = {"ex": zz * 2 + (1 - w)}
    across_x = {"grp": (grp // 2) * 2 + (1 - side)}
    across_c = {"lay": 1 - core}
    has_left = zz > 0
    has_right = zz < line - 1
    lefts = zz
    rights = line - 1 - zz
    both_ways = jnp.minimum(lefts, rights)

    def z_chunk(k):
        return jnp.where(
            k < 2, 2 * side + k, jnp.where(k == 2, 4 + side, jnp.where(k < 5, 3 + k, 5 - side))
        )

    def own_chunk(k):
        return jnp.where(k < 2, 2 * side + k, jnp.where(k == 2, 4 + side, 6 + side))

    def remote(src, dst, send, recv, target):
        return pltpu.make_async_remote_copy(
            src_ref=src, dst_ref=dst, send_sem=send, recv_sem=recv,
            device_id=target, device_id_type=MESH,
        )

    def load(p):
        return pltpu.make_async_copy(
            train_ref.at[:, pl.ds(p * wide, wide)], stored.at[p], load_sem.at[p]
        )

    def z_copy(b, k, send, target):
        slot = held.at[b, z_chunk(k), w]
        return remote(slot, slot, send.at[b], z_recv.at[b, k], target)

    def y_copy(b, k, c, column):
        slot = held.at[b, c, column]
        return remote(slot, slot, y_send.at[b], y_recv.at[b, k], across_y)

    def x_copy(b, k, c, column):
        slot = held.at[b, c, column]
        return remote(slot, slot, x_send.at[b], x_recv.at[b, k], across_x)

    def c_copy(b):
        return remote(acc.at[b, 1 - core], arrived.at[b], c_send.at[b], c_recv.at[b], across_c)

    def out_copy(b):
        return pltpu.make_async_copy(total.at[b], out_ref.at[b], out_sem.at[b])

    def block_of(j):
        i = j - 1
        paired = i < 2 * both_ways
        t = jnp.where(paired, i // 2 + 1, j - both_ways)
        from_left = jnp.where(paired, jnp.asarray(i % 2 == 0).astype(jnp.int32), (lefts > rights).astype(jnp.int32))
        return jnp.where(from_left > 0, zz - t, zz + t)

    @pl.loop(0, loads)
    def _(p):
        load(p).start()

    barrier = pltpu.get_barrier_semaphore()

    @pl.when(has_left)
    def _():
        pl.semaphore_signal(barrier, inc=1, device_id=left, device_id_type=MESH)

    @pl.when(has_right)
    def _():
        pl.semaphore_signal(barrier, inc=1, device_id=right, device_id_type=MESH)

    for target in (across_y, across_x, across_c):
        pl.semaphore_signal(barrier, inc=1, device_id=target, device_id_type=MESH)

    own = pltpu.make_async_copy(own_ref, held.at[zz, :, w], own_sem)
    own.start()
    own.wait()
    pl.semaphore_wait(barrier, 3 + has_left.astype(jnp.int32) + has_right.astype(jnp.int32))

    @pl.loop(0, 6)
    def _(k):
        @pl.when(has_right)
        def _():
            z_copy(zz, k, zr_send, right).start()

        @pl.when(has_left)
        def _():
            z_copy(zz, k, zl_send, left).start()

        @pl.when(k < 4)
        def _():
            y_copy(zz, k, own_chunk(k), w).start()

    spread = jnp.broadcast_to(ids_ref[...].astype(jnp.float32), (128, examples)).T
    lanes = lax.broadcasted_iota(jnp.int32, (examples, 128), 1).astype(jnp.float32)
    for tile in range(examples // 128):
        hot[:, tile * 128:(tile + 1) * 128] = jnp.where(
            spread == lanes + float(tile * 128), 1.0, 0.0
        ).astype(jnp.bfloat16)

    def z_arrival(b, k, from_left):
        z_copy(b, k, zr_send, right).wait_recv()
        if from_left:
            @pl.when(has_right)
            def _():
                z_copy(b, k, zr_send, right).start()
        else:
            @pl.when(has_left)
            def _():
                z_copy(b, k, zl_send, left).start()

        @pl.when(k < 5)
        def _():
            y_copy(b, k, z_chunk(k), w).start()

        @pl.when(k < 2)
        def _():
            x_copy(b, k, z_chunk(k), w).start()

    def relay(tick):
        t = tick // 6 + 1
        k = tick % 6

        @pl.when(jnp.logical_and(t < line, zz - t >= 0))
        def _():
            z_arrival(zz - t, k, True)

        @pl.when(jnp.logical_and(t < line, zz + t < line))
        def _():
            z_arrival(zz + t, k, False)

        q = tick - 1

        @pl.when(jnp.logical_and(q >= 0, q < 4))
        def _():
            y_copy(zz, q, own_chunk(q), 1 - w).wait_recv()
            x_copy(zz, q, own_chunk(q), 1 - w).start()

        @pl.when(jnp.logical_and(q >= 4, q < 4 + 5 * (line - 1)))
        def _():
            b = block_of((q - 4) // 5 + 1)
            k = (q - 4) % 5
            y_copy(b, k, z_chunk(k), 1 - w).wait_recv()

            @pl.when(k < 3)
            def _():
                x_copy(b, k + 2, z_chunk(k), 1 - w).start()

    def permute(c):
        p = c // per_load
        at = c % per_load

        @pl.when(at == 0)
        def _():
            load(p).wait()

        columns = pl.ds(pl.multiple_of(at * chunk, chunk), chunk)

        @pl.loop(0, 4)
        def _(part):
            quarter = examples // 4
            picked = pl.ds(part * quarter, quarter)
            perm[c, picked, :] = jnp.dot(
                hot[picked, :], stored[p, :, columns], preferred_element_type=jnp.float32
            ).astype(jnp.bfloat16)

    per_half = half // window

    def terms(b, n, picked):
        part = pl.ds(pl.multiple_of(n * window, window), window)
        value = None
        for c in picked:
            term = lax.dot_general(
                held[b, c].reshape(2 * rows, chunk), perm[c, part, :],
                (((1,), (1,)), ((), ())), preferred_element_type=jnp.float32,
            )
            value = term if value is None else value + term
        return value

    def columns_of(n):
        return n // per_half, pl.ds(pl.multiple_of((n % per_half) * window, window), window)

    def whole_block(b, n):
        h, at = columns_of(n)
        acc[b, h, :, at] = terms(b, n, range(chunks))

    def x_arrivals(b, first, last):
        for k in range(first, last):
            x_copy(b, k, 0, w).wait_recv()

    def finish(b):
        c_copy(b).wait_recv()
        total[b] = acc[b, core] + arrived[b]
        out_copy(b).start()

    tiles = examples // window
    first_own = 8

    def compute(tick):
        @pl.when(tick < chunks)
        def _():
            permute(tick)

        for at in range(2):
            @pl.when(tick == first_own + at)
            def _():
                if at == 0:
                    x_arrivals(zz, 0, 4)

                @pl.loop(at * (tiles // 2), (at + 1) * (tiles // 2))
                def _(n):
                    whole_block(zz, n)

                if at == 1:
                    c_copy(zz).start()

            j = (tick - 6 - at) // 6

            @pl.when(jnp.logical_and(tick % 6 == at, jnp.logical_and(tick >= 12, j < line - 1)))
            def _():
                b = block_of(j)
                if at == 0:
                    x_arrivals(b, 0, 5)

                @pl.loop(at * (tiles // 2), (at + 1) * (tiles // 2))
                def _(n):
                    whole_block(b, n)

                if at == 1:
                    c_copy(b).start()

    ticks = max(6 * (line - 1), 5 * line, 6 * (line - 2) + 8)

    @pl.loop(0, ticks)
    def _(tick):
        relay(tick)
        compute(tick)

    last = block_of(line - 1)
    mine = (2 * side, 2 * side + 1, 4 + side, 6, 7)
    pair = (2 - 2 * side, 3 - 2 * side)
    single = (5 - side,)

    @pl.loop(0, tiles)
    def _(n):
        h, at = columns_of(n)
        acc[last, h, :, at] = terms(last, n, mine)

    @pl.loop(0, line)
    def _(b):
        @pl.when(b != last)
        def _():
            finish(b)

    x_arrivals(last, 0, 4)

    @pl.loop(0, tiles)
    def _(n):
        h, at = columns_of(n)
        acc[last, h, :, at] = acc[last, h, :, at] + terms(last, n, pair)

    x_arrivals(last, 4, 5)

    @pl.loop(0, tiles)
    def _(n):
        h, at = columns_of(n)
        acc[last, h, :, at] = acc[last, h, :, at] + terms(last, n, single)

    c_copy(last).start()
    finish(last)

    def sent(b, count, send):
        span = held.at[b, pl.ds(0, count), w]
        remote(span, span, send.at[b], z_recv.at[b, 0], across_y).wait_send()

    @pl.loop(0, line)
    def _(b):
        @pl.when(jnp.logical_and(has_right, b <= zz))
        def _():
            sent(b, 6, zr_send)

        @pl.when(jnp.logical_and(has_left, b >= zz))
        def _():
            sent(b, 6, zl_send)

        @pl.when(b == zz)
        def _():
            sent(b, 4, y_send)
            sent(b, 4, x_send)

        @pl.when(b != zz)
        def _():
            sent(b, 5, y_send)
            sent(b, 5, x_send)

        c_copy(b).wait_send()
        out_copy(b).wait()


def scores_of(own, ids, train, devices):
    rows = own.shape[1]
    chunk = own.shape[2]
    examples = train.shape[0]
    line = devices // 2
    dma = pltpu.SemaphoreType.DMA
    return pl.pallas_call(
        functools.partial(score_kernel, line),
        out_shape=jax.ShapeDtypeStruct((line, 2 * rows, examples // 2), jnp.float32),
        in_specs=[
            pl.BlockSpec(memory_space=pltpu.VMEM),
            pl.BlockSpec(memory_space=pltpu.VMEM),
            pl.BlockSpec(memory_space=pl.ANY),
        ],
        out_specs=pl.BlockSpec(memory_space=pl.ANY),
        scratch_shapes=[
            pltpu.VMEM((loads, examples, train.shape[1] // loads), jnp.bfloat16),
            pltpu.VMEM((examples, examples), jnp.bfloat16),
            pltpu.VMEM((chunks, examples, chunk), jnp.bfloat16),
            pltpu.VMEM((line, chunks, 2, rows, chunk), jnp.bfloat16),
            pltpu.VMEM((line, 2, 2 * rows, examples // 2), jnp.float32),
            pltpu.VMEM((line, 2 * rows, examples // 2), jnp.float32),
            pltpu.VMEM((line, 2 * rows, examples // 2), jnp.float32),
            dma((loads,)),
            dma,
            dma((line, 6)),
            dma((line, 5)),
            dma((line, 5)),
            *[dma((line,)) for _ in range(7)],
        ],
        compiler_params=pltpu.CompilerParams(
            collective_id=0, has_side_effects=True, vmem_limit_bytes=56 * 1024 * 1024
        ),
    )(own, ids, train)


def shards(devices, queries, basis_s, basis_a, eigvals, train_grads, example_ids):
    stored = train_grads.reshape(train_grads.shape[0], -1)
    own_rows = precondition(queries, basis_s, basis_a, eigvals)
    rows = own_rows.shape[0]
    cut = own_rows.reshape(rows, chunks, -1).transpose(1, 0, 2)
    scores = scores_of(cut, example_ids, stored, devices)
    return scores.reshape(devices * rows, -1)


def solution(mesh):
    return jax.shard_map(
        functools.partial(shards, mesh.shape["ex"]),
        mesh=mesh,
        in_specs=(
            P("ex", "lay", None),
            P("lay", None, None),
            P("lay", None, None),
            P("lay", None, None),
            P(("grp", "ex"), "lay", None),
            P(("grp", "ex"), None),
        ),
        out_specs=P(None, ("grp", "ex", "lay")),
        check_vma=False,
    )
```

```python
import functools

import jax
import jax.numpy as jnp
from jax import lax
from jax.experimental import pallas as pl
from jax.experimental.pallas import tpu as pltpu
from jax.sharding import PartitionSpec as P

damp_ratio = 0.1
chunks = 8
loads = 4
window = 256
MESH = pl.DeviceIdType.MESH


def split(value):
    top = value.astype(jnp.bfloat16)
    return top, (value - top.astype(jnp.float32)).astype(jnp.bfloat16)


def ones_where(mask):
    return jnp.where(mask, 1.0, 0.0).astype(jnp.bfloat16)


def picks(shape, rule):
    return ones_where(rule(lax.broadcasted_iota(jnp.int32, shape, 0), lax.broadcasted_iota(jnp.int32, shape, 1)))


def product(a, b, dims=((1,), (0,))):
    return lax.dot_general(a, b, (dims, ((), ())), preferred_element_type=jnp.float32)


across = ((1,), (1,))


def twice_diagonal(part, rank):
    spread = product(part, picks((rank, 2 * rank), lambda r, c: r == c % rank))
    both = jnp.concatenate([spread, spread], axis=0)
    shape = (2 * rank, 2 * rank)
    same = lax.broadcasted_iota(jnp.int32, shape, 0) // rank == lax.broadcasted_iota(jnp.int32, shape, 1) // rank
    return jnp.where(same, both, 0.0).astype(jnp.bfloat16)


def rotate(queries_ref, s_ref, a_ref, eig_ref, turned, stacked):
    rows = queries_ref.shape[0]
    rank = s_ref.shape[0]
    half = rank // 2
    lane = 2 * rank
    a_top, a_low = (twice_diagonal(part, rank) for part in split(a_ref[...]))
    a_both = jnp.concatenate([a_top, a_low], axis=0)
    for i in range(half):
        tile = queries_ref[:, i * lane:(i + 1) * lane]
        turned[i * rows:(i + 1) * rows, :] = product(jnp.concatenate([tile, tile], axis=1), a_both)

    eye = picks((rank, rank), lambda r, c: r == c)
    s_parts = split(s_ref[...])
    forward = []
    back = []
    for top_or_low, part in enumerate(s_parts):
        flipped = product(eye, part, across).astype(jnp.bfloat16)
        sorted_rows = product(picks((rank, rank), lambda r, c: c == (r % half) * 2 + r // half), part).astype(jnp.bfloat16)

        def wanted(c):
            third = c // half
            return third < 2 if top_or_low == 0 else third == 2

        forward.append([
            product(flipped, picks((rank, 3 * half), lambda r, c: (r == 2 * (c % half) + b) & wanted(c)))
            for b in range(2)
        ])
        back.append([
            product(sorted_rows, picks((rank, 3 * half), lambda r, c: (r == c % half + b * half) & wanted(c)))
            for b in range(2)
        ])
    lhs_forward = jnp.concatenate([forward[0][b] + forward[1][b] for b in range(2)], axis=0).astype(jnp.bfloat16)
    lhs_back = jnp.concatenate([back[0][b] + back[1][b] for b in range(2)], axis=0).astype(jnp.bfloat16)

    eig = eig_ref[...]
    damping = damp_ratio * jnp.mean(eig)
    inverse = 1.0 / (jnp.concatenate([eig[:half], eig[half:]], axis=1) + damping)
    first = lax.broadcasted_iota(jnp.int32, (half, lane), 1) < rank

    def gather_halves(value):
        kept = jnp.where(first, value[:half], value[3 * half:])
        crossed = jnp.where(first, value[half:2 * half], value[2 * half:3 * half])
        return kept + pltpu.roll(crossed, rank, 1)

    def stack(at, value):
        top, low = split(value)
        stacked[0:half, at] = top
        stacked[half:2 * half, at] = low
        stacked[2 * half:3 * half, at] = top

    group = 8
    for base in range(0, rows, group):
        for n in range(base, base + group):
            stack(slice(n * lane, (n + 1) * lane), turned[pl.ds(n, half, stride=rows), :])
    for base in range(0, rows, group):
        span = slice(base * lane, (base + group) * lane)
        value = product(lhs_forward, stacked[:, span])
        for n in range(group):
            scaled = gather_halves(value[:, n * lane:(n + 1) * lane]) * inverse
            stack(slice((base + n) * lane, (base + n + 1) * lane), scaled)
    for base in range(0, rows, group):
        span = slice(base * lane, (base + group) * lane)
        value = product(lhs_back, stacked[:, span])
        for n in range(group):
            turned[pl.ds(base + n, half, stride=rows), :] = gather_halves(value[:, n * lane:(n + 1) * lane])
    return jnp.concatenate([a_top, a_top, a_low], axis=1)


def condition_chunk(turned, c, rows, per_chunk, a_all, write):
    lane = turned.shape[1]
    top, low = split(turned[pl.ds(pl.multiple_of(c * per_chunk * rows, 8), per_chunk * rows), :])
    value = product(jnp.concatenate([top, low, top], axis=1), a_all, across).astype(jnp.bfloat16)
    for i in range(per_chunk):
        write(slice(i * lane, (i + 1) * lane), value[i * rows:(i + 1) * rows])

def score_kernel(
    line, queries_ref, s_ref, a_ref, eig_ref, ids_ref, train_ref, out_ref,
    turned, stacked, stored, hot, perm, held, acc, arrived, total,
    load_sem, z_recv, y_recv, x_recv, zr_send, zl_send, y_send, x_send, c_recv, c_send, out_sem,
):
    grp = lax.axis_index("grp")
    ex = lax.axis_index("ex")
    core = lax.axis_index("lay")
    zz = ex // 2
    w = ex % 2
    side = grp % 2
    rows = queries_ref.shape[0]
    examples = train_ref.shape[0]
    chunk = queries_ref.shape[1] // chunks
    half = examples // 2
    wide = train_ref.shape[1] // loads
    per_load = chunks // loads
    right = {"ex": lax.rem(ex + 2, 2 * line)}
    left = {"ex": lax.rem(ex + 2 * line - 2, 2 * line)}
    across_y = {"ex": zz * 2 + (1 - w)}
    across_x = {"grp": (grp // 2) * 2 + (1 - side)}
    across_c = {"lay": 1 - core}
    has_left = zz > 0
    has_right = zz < line - 1
    lefts = zz
    rights = line - 1 - zz
    both_ways = jnp.minimum(lefts, rights)

    def z_chunk(k):
        return jnp.where(
            k < 2, 2 * side + k, jnp.where(k == 2, 4 + side, jnp.where(k < 5, 3 + k, 5 - side))
        )

    def own_chunk(k):
        return jnp.where(k < 2, 2 * side + k, jnp.where(k == 2, 4 + side, 6 + side))

    def remote(src, dst, send, recv, target):
        return pltpu.make_async_remote_copy(
            src_ref=src, dst_ref=dst, send_sem=send, recv_sem=recv,
            device_id=target, device_id_type=MESH,
        )

    def load(p):
        return pltpu.make_async_copy(
            train_ref.at[:, pl.ds(p * wide, wide)], stored.at[p], load_sem.at[p]
        )

    def z_copy(b, k, send, target):
        slot = held.at[b, z_chunk(k), w]
        return remote(slot, slot, send.at[b], z_recv.at[b, k], target)

    def y_copy(b, k, c, column):
        slot = held.at[b, c, column]
        return remote(slot, slot, y_send.at[b], y_recv.at[b, k], across_y)

    def x_copy(b, k, c, column):
        slot = held.at[b, c, column]
        return remote(slot, slot, x_send.at[b], x_recv.at[b, k], across_x)

    def c_copy(b):
        return remote(acc.at[b, 1 - core], arrived.at[b], c_send.at[b], c_recv.at[b], across_c)

    def out_copy(b):
        return pltpu.make_async_copy(total.at[b], out_ref.at[b], out_sem.at[b])

    def block_of(j):
        i = j - 1
        paired = i < 2 * both_ways
        t = jnp.where(paired, i // 2 + 1, j - both_ways)
        from_left = jnp.where(paired, jnp.asarray(i % 2 == 0).astype(jnp.int32), (lefts > rights).astype(jnp.int32))
        return jnp.where(from_left > 0, zz - t, zz + t)

    @pl.loop(0, loads)
    def _(p):
        load(p).start()

    barrier = pltpu.get_barrier_semaphore()

    @pl.when(has_left)
    def _():
        pl.semaphore_signal(barrier, inc=1, device_id=left, device_id_type=MESH)

    @pl.when(has_right)
    def _():
        pl.semaphore_signal(barrier, inc=1, device_id=right, device_id_type=MESH)

    for target in (across_y, across_x, across_c):
        pl.semaphore_signal(barrier, inc=1, device_id=target, device_id_type=MESH)

    a_all = rotate(queries_ref, s_ref, a_ref, eig_ref, turned, stacked)

    def condition(c):
        def write(at, value):
            held[zz, c, w, :, at] = value

        condition_chunk(turned, c, rows, chunk // turned.shape[1], a_all, write)

    pl.semaphore_wait(barrier, 3 + has_left.astype(jnp.int32) + has_right.astype(jnp.int32))

    @pl.loop(0, 6)
    def _(k):
        condition(z_chunk(k))

        @pl.when(has_right)
        def _():
            z_copy(zz, k, zr_send, right).start()

        @pl.when(has_left)
        def _():
            z_copy(zz, k, zl_send, left).start()

        @pl.when(k < 3)
        def _():
            y_copy(zz, k, own_chunk(k), w).start()

        @pl.when(k == 4)
        def _():
            y_copy(zz, 3, own_chunk(3), w).start()

    @pl.loop(0, 2)
    def _(k):
        condition(2 - 2 * side + k)

    spread = jnp.broadcast_to(ids_ref[...].astype(jnp.float32), (128, examples)).T
    lanes = lax.broadcasted_iota(jnp.int32, (examples, 128), 1).astype(jnp.float32)
    for tile in range(examples // 128):
        hot[:, tile * 128:(tile + 1) * 128] = jnp.where(
            spread == lanes + float(tile * 128), 1.0, 0.0
        ).astype(jnp.bfloat16)

    def z_arrival(b, k, from_left):
        z_copy(b, k, zr_send, right).wait_recv()
        if from_left:
            @pl.when(has_right)
            def _():
                z_copy(b, k, zr_send, right).start()
        else:
            @pl.when(has_left)
            def _():
                z_copy(b, k, zl_send, left).start()

        @pl.when(k < 5)
        def _():
            y_copy(b, k, z_chunk(k), w).start()

        @pl.when(k < 2)
        def _():
            x_copy(b, k, z_chunk(k), w).start()

    def relay(tick):
        t = tick // 6 + 1
        k = tick % 6

        @pl.when(jnp.logical_and(t < line, zz - t >= 0))
        def _():
            z_arrival(zz - t, k, True)

        @pl.when(jnp.logical_and(t < line, zz + t < line))
        def _():
            z_arrival(zz + t, k, False)

        q = tick - 1

        @pl.when(jnp.logical_and(q >= 0, q < 4))
        def _():
            y_copy(zz, q, own_chunk(q), 1 - w).wait_recv()
            x_copy(zz, q, own_chunk(q), 1 - w).start()

        @pl.when(jnp.logical_and(q >= 4, q < 4 + 5 * (line - 1)))
        def _():
            b = block_of((q - 4) // 5 + 1)
            k = (q - 4) % 5
            y_copy(b, k, z_chunk(k), 1 - w).wait_recv()

            @pl.when(k < 3)
            def _():
                x_copy(b, k + 2, z_chunk(k), 1 - w).start()

    def permute(c):
        p = c // per_load
        at = c % per_load

        @pl.when(at == 0)
        def _():
            load(p).wait()

        columns = pl.ds(pl.multiple_of(at * chunk, chunk), chunk)

        @pl.loop(0, 4)
        def _(part):
            quarter = examples // 4
            picked = pl.ds(part * quarter, quarter)
            perm[c, picked, :] = jnp.dot(
                hot[picked, :], stored[p, :, columns], preferred_element_type=jnp.float32
            ).astype(jnp.bfloat16)

    per_half = half // window

    def terms(b, n, picked):
        part = pl.ds(pl.multiple_of(n * window, window), window)
        value = None
        for c in picked:
            term = lax.dot_general(
                held[b, c].reshape(2 * rows, chunk), perm[c, part, :],
                (((1,), (1,)), ((), ())), preferred_element_type=jnp.float32,
            )
            value = term if value is None else value + term
        return value

    def columns_of(n):
        return n // per_half, pl.ds(pl.multiple_of((n % per_half) * window, window), window)

    def whole_block(b, n):
        h, at = columns_of(n)
        acc[b, h, :, at] = terms(b, n, range(chunks))

    def x_arrivals(b, first, last):
        for k in range(first, last):
            x_copy(b, k, 0, w).wait_recv()

    def finish(b):
        c_copy(b).wait_recv()
        total[b] = acc[b, core] + arrived[b]
        out_copy(b).start()

    tiles = examples // window
    first_own = 8

    def compute(tick):
        @pl.when(tick < chunks)
        def _():
            permute(tick)

        for at in range(2):
            @pl.when(tick == first_own + at)
            def _():
                if at == 0:
                    x_arrivals(zz, 0, 4)

                @pl.loop(at * (tiles // 2), (at + 1) * (tiles // 2))
                def _(n):
                    whole_block(zz, n)

                if at == 1:
                    c_copy(zz).start()

            j = (tick - 6 - at) // 6

            @pl.when(jnp.logical_and(tick % 6 == at, jnp.logical_and(tick >= 12, j < line - 1)))
            def _():
                b = block_of(j)
                if at == 0:
                    x_arrivals(b, 0, 5)

                @pl.loop(at * (tiles // 2), (at + 1) * (tiles // 2))
                def _(n):
                    whole_block(b, n)

                if at == 1:
                    c_copy(b).start()

    ticks = max(6 * (line - 1), 5 * line, 6 * (line - 2) + 8)

    @pl.loop(0, ticks)
    def _(tick):
        relay(tick)
        compute(tick)

    last = block_of(line - 1)
    mine = (2 * side, 2 * side + 1, 4 + side, 6, 7)
    pair = (2 - 2 * side, 3 - 2 * side)
    single = (5 - side,)

    @pl.loop(0, tiles)
    def _(n):
        h, at = columns_of(n)
        acc[last, h, :, at] = terms(last, n, mine)

    @pl.loop(0, line)
    def _(b):
        @pl.when(b != last)
        def _():
            finish(b)

    x_arrivals(last, 0, 4)

    @pl.loop(0, tiles)
    def _(n):
        h, at = columns_of(n)
        acc[last, h, :, at] = acc[last, h, :, at] + terms(last, n, pair)

    x_arrivals(last, 4, 5)

    @pl.loop(0, tiles)
    def _(n):
        h, at = columns_of(n)
        acc[last, h, :, at] = acc[last, h, :, at] + terms(last, n, single)

    c_copy(last).start()
    finish(last)

    def sent(b, count, send):
        span = held.at[b, pl.ds(0, count), w]
        remote(span, span, send.at[b], z_recv.at[b, 0], across_y).wait_send()

    @pl.loop(0, line)
    def _(b):
        @pl.when(jnp.logical_and(has_right, b <= zz))
        def _():
            sent(b, 6, zr_send)

        @pl.when(jnp.logical_and(has_left, b >= zz))
        def _():
            sent(b, 6, zl_send)

        @pl.when(b == zz)
        def _():
            sent(b, 4, y_send)
            sent(b, 4, x_send)

        @pl.when(b != zz)
        def _():
            sent(b, 5, y_send)
            sent(b, 5, x_send)

        c_copy(b).wait_send()
        out_copy(b).wait()


def scores_of(queries, basis_s, basis_a, eigvals, ids, train, devices):
    rows = queries.shape[0]
    chunk = queries.shape[1] // chunks
    rank = basis_s.shape[0]
    examples = train.shape[0]
    line = devices // 2
    dma = pltpu.SemaphoreType.DMA
    vmem = pl.BlockSpec(memory_space=pltpu.VMEM)
    return pl.pallas_call(
        functools.partial(score_kernel, line),
        out_shape=jax.ShapeDtypeStruct((line, 2 * rows, examples // 2), jnp.float32),
        in_specs=[vmem] * 5 + [pl.BlockSpec(memory_space=pl.ANY)],
        out_specs=pl.BlockSpec(memory_space=pl.ANY),
        scratch_shapes=[
            pltpu.VMEM((rank // 2 * rows, 2 * rank), jnp.float32),
            pltpu.VMEM((3 * rank // 2, rows * 2 * rank), jnp.bfloat16),
            pltpu.VMEM((loads, examples, train.shape[1] // loads), jnp.bfloat16),
            pltpu.VMEM((examples, examples), jnp.bfloat16),
            pltpu.VMEM((chunks, examples, chunk), jnp.bfloat16),
            pltpu.VMEM((line, chunks, 2, rows, chunk), jnp.bfloat16),
            pltpu.VMEM((line, 2, 2 * rows, examples // 2), jnp.float32),
            pltpu.VMEM((line, 2 * rows, examples // 2), jnp.float32),
            pltpu.VMEM((line, 2 * rows, examples // 2), jnp.float32),
            dma((loads,)),
            dma((line, 6)),
            dma((line, 5)),
            dma((line, 5)),
            *[dma((line,)) for _ in range(7)],
        ],
        compiler_params=pltpu.CompilerParams(
            collective_id=0, has_side_effects=True, vmem_limit_bytes=56 * 1024 * 1024
        ),
    )(queries, basis_s, basis_a, eigvals, ids, train)


def shards(devices, queries, basis_s, basis_a, eigvals, train_grads, example_ids):
    scores = scores_of(
        queries.reshape(queries.shape[0], -1), basis_s[0], basis_a[0], eigvals[0],
        example_ids, train_grads.reshape(train_grads.shape[0], -1), devices,
    )
    return scores.reshape(devices * queries.shape[0], -1)


def solution(mesh):
    return jax.shard_map(
        functools.partial(shards, mesh.shape["ex"]),
        mesh=mesh,
        in_specs=(
            P("ex", "lay", None),
            P("lay", None, None),
            P("lay", None, None),
            P("lay", None, None),
            P(("grp", "ex"), "lay", None),
            P(("grp", "ex"), None),
        ),
        out_specs=P(None, ("grp", "ex", "lay")),
        check_vma=False,
    )
```

```python
import functools

import jax
import jax.numpy as jnp
from jax import lax
from jax.experimental import pallas as pl
from jax.experimental.pallas import tpu as pltpu
from jax.sharding import PartitionSpec as P

damp_ratio = 0.1
chunks = 8
slices = 4
MESH = pl.DeviceIdType.MESH


def split(value):
    top = value.astype(jnp.bfloat16)
    return top, (value - top.astype(jnp.float32)).astype(jnp.bfloat16)


def ones_where(mask):
    return jnp.where(mask, 1.0, 0.0).astype(jnp.bfloat16)


def picks(shape, rule):
    return ones_where(rule(lax.broadcasted_iota(jnp.int32, shape, 0), lax.broadcasted_iota(jnp.int32, shape, 1)))


def product(a, b, dims=((1,), (0,))):
    return lax.dot_general(a, b, (dims, ((), ())), preferred_element_type=jnp.float32)


across = ((1,), (1,))


def twice_diagonal(part, rank):
    spread = product(part, picks((rank, 2 * rank), lambda r, c: r == c % rank))
    both = jnp.concatenate([spread, spread], axis=0)
    shape = (2 * rank, 2 * rank)
    same = lax.broadcasted_iota(jnp.int32, shape, 0) // rank == lax.broadcasted_iota(jnp.int32, shape, 1) // rank
    return jnp.where(same, both, 0.0).astype(jnp.bfloat16)


def rotate(queries_ref, s_ref, a_ref, eig_ref, turned, stacked):
    rows = queries_ref.shape[0]
    rank = s_ref.shape[0]
    half = rank // 2
    lane = 2 * rank
    a_top, a_low = (twice_diagonal(part, rank) for part in split(a_ref[...]))
    a_both = jnp.concatenate([a_top, a_low], axis=0)
    for i in range(half):
        tile = queries_ref[:, i * lane:(i + 1) * lane]
        turned[i * rows:(i + 1) * rows, :] = product(jnp.concatenate([tile, tile], axis=1), a_both)

    eye = picks((rank, rank), lambda r, c: r == c)
    s_parts = split(s_ref[...])
    forward = []
    back = []
    for top_or_low, part in enumerate(s_parts):
        flipped = product(eye, part, across).astype(jnp.bfloat16)
        sorted_rows = product(picks((rank, rank), lambda r, c: c == (r % half) * 2 + r // half), part).astype(jnp.bfloat16)

        def wanted(c):
            third = c // half
            return third < 2 if top_or_low == 0 else third == 2

        forward.append([
            product(flipped, picks((rank, 3 * half), lambda r, c: (r == 2 * (c % half) + b) & wanted(c)))
            for b in range(2)
        ])
        back.append([
            product(sorted_rows, picks((rank, 3 * half), lambda r, c: (r == c % half + b * half) & wanted(c)))
            for b in range(2)
        ])
    lhs_forward = jnp.concatenate([forward[0][b] + forward[1][b] for b in range(2)], axis=0).astype(jnp.bfloat16)
    lhs_back = jnp.concatenate([back[0][b] + back[1][b] for b in range(2)], axis=0).astype(jnp.bfloat16)

    eig = eig_ref[...]
    damping = damp_ratio * jnp.mean(eig)
    inverse = 1.0 / (jnp.concatenate([eig[:half], eig[half:]], axis=1) + damping)
    first = lax.broadcasted_iota(jnp.int32, (half, lane), 1) < rank

    def gather_halves(value):
        kept = jnp.where(first, value[:half], value[3 * half:])
        crossed = jnp.where(first, value[half:2 * half], value[2 * half:3 * half])
        return kept + pltpu.roll(crossed, rank, 1)

    def stack(at, value):
        top, low = split(value)
        stacked[0:half, at] = top
        stacked[half:2 * half, at] = low
        stacked[2 * half:3 * half, at] = top

    group = 8
    for base in range(0, rows, group):
        for n in range(base, base + group):
            stack(slice(n * lane, (n + 1) * lane), turned[pl.ds(n, half, stride=rows), :])
    for base in range(0, rows, group):
        span = slice(base * lane, (base + group) * lane)
        value = product(lhs_forward, stacked[:, span])
        for n in range(group):
            scaled = gather_halves(value[:, n * lane:(n + 1) * lane]) * inverse
            stack(slice((base + n) * lane, (base + n + 1) * lane), scaled)
    for base in range(0, rows, group):
        span = slice(base * lane, (base + group) * lane)
        value = product(lhs_back, stacked[:, span])
        for n in range(group):
            turned[pl.ds(base + n, half, stride=rows), :] = gather_halves(value[:, n * lane:(n + 1) * lane])
    return jnp.concatenate([a_top, a_top, a_low], axis=1)


def condition_chunk(turned, c, rows, per_chunk, a_all, write):
    lane = turned.shape[1]
    top, low = split(turned[pl.ds(pl.multiple_of(c * per_chunk * rows, 8), per_chunk * rows), :])
    value = product(jnp.concatenate([top, low, top], axis=1), a_all, across).astype(jnp.bfloat16)
    for i in range(per_chunk):
        write(slice(i * lane, (i + 1) * lane), value[i * rows:(i + 1) * rows])

def score_kernel(
    line, queries_ref, s_ref, a_ref, eig_ref, ids_ref, train_ref, out_ref,
    turned, stacked, stored, hot, held, acc, arrived, total,
    load_sem, z_recv, y_recv, x_recv, zr_send, zl_send, y_send, x_send, c_recv, c_send, out_sem,
):
    grp = lax.axis_index("grp")
    ex = lax.axis_index("ex")
    core = lax.axis_index("lay")
    zz = ex // 2
    w = ex % 2
    side = grp % 2
    rows = queries_ref.shape[0]
    examples = train_ref.shape[0]
    chunk = queries_ref.shape[1] // chunks
    half = examples // 2
    window = examples // slices
    right = {"ex": lax.rem(ex + 2, 2 * line)}
    left = {"ex": lax.rem(ex + 2 * line - 2, 2 * line)}
    across_y = {"ex": zz * 2 + (1 - w)}
    across_x = {"grp": (grp // 2) * 2 + (1 - side)}
    across_c = {"lay": 1 - core}
    has_left = zz > 0
    has_right = zz < line - 1
    lefts = zz
    rights = line - 1 - zz
    both_ways = jnp.minimum(lefts, rights)

    def z_chunk(k):
        return jnp.where(
            k < 2, 2 * side + k, jnp.where(k == 2, 4 + side, jnp.where(k < 5, 3 + k, 5 - side))
        )

    def own_chunk(k):
        return jnp.where(k < 2, 2 * side + k, jnp.where(k == 2, 4 + side, 6 + side))

    def remote(src, dst, send, recv, target):
        return pltpu.make_async_remote_copy(
            src_ref=src, dst_ref=dst, send_sem=send, recv_sem=recv,
            device_id=target, device_id_type=MESH,
        )

    def load(c):
        return pltpu.make_async_copy(
            train_ref.at[:, pl.ds(c * chunk, chunk)], stored.at[c], load_sem
        )

    def z_copy(b, k, send, target):
        slot = held.at[b, z_chunk(k), w]
        return remote(slot, slot, send.at[b], z_recv.at[b, k], target)

    def y_copy(b, k, c, column):
        slot = held.at[b, c, column]
        return remote(slot, slot, y_send.at[b], y_recv.at[b, k], across_y)

    def x_copy(b, k, c, column):
        slot = held.at[b, c, column]
        return remote(slot, slot, x_send.at[b], x_recv.at[b, k], across_x)

    def c_copy(b):
        return remote(acc.at[b], arrived.at[b], c_send.at[b], c_recv.at[b], across_c)

    def out_copy(b):
        return pltpu.make_async_copy(total.at[b], out_ref.at[b], out_sem.at[b])

    def block_of(j):
        i = j - 1
        paired = i < 2 * both_ways
        t = jnp.where(paired, i // 2 + 1, j - both_ways)
        from_left = jnp.where(paired, jnp.asarray(i % 2 == 0).astype(jnp.int32), (lefts > rights).astype(jnp.int32))
        return jnp.where(from_left > 0, zz - t, zz + t)

    @pl.loop(0, chunks)
    def _(c):
        load(c).start()

    barrier = pltpu.get_barrier_semaphore()

    @pl.when(has_left)
    def _():
        pl.semaphore_signal(barrier, inc=1, device_id=left, device_id_type=MESH)

    @pl.when(has_right)
    def _():
        pl.semaphore_signal(barrier, inc=1, device_id=right, device_id_type=MESH)

    for target in (across_y, across_x, across_c):
        pl.semaphore_signal(barrier, inc=1, device_id=target, device_id_type=MESH)

    a_all = rotate(queries_ref, s_ref, a_ref, eig_ref, turned, stacked)

    def condition(c):
        def write(at, value):
            held[zz, c, w, :, at] = value

        condition_chunk(turned, c, rows, chunk // turned.shape[1], a_all, write)

    pl.semaphore_wait(barrier, 3 + has_left.astype(jnp.int32) + has_right.astype(jnp.int32))

    @pl.loop(0, 6)
    def _(k):
        condition(z_chunk(k))

        @pl.when(has_right)
        def _():
            z_copy(zz, k, zr_send, right).start()

        @pl.when(has_left)
        def _():
            z_copy(zz, k, zl_send, left).start()

        @pl.when(k < 3)
        def _():
            y_copy(zz, k, own_chunk(k), w).start()

        @pl.when(k == 4)
        def _():
            y_copy(zz, 3, own_chunk(3), w).start()

    @pl.loop(0, 2)
    def _(k):
        condition(2 - 2 * side + k)

    ids = ids_ref[...].astype(jnp.float32)
    wanted = jnp.where(core == 0, ids[:, :half], ids[:, half:])
    for tile in range(examples // 128):
        row = lax.broadcasted_iota(jnp.int32, (128, half), 0).astype(jnp.float32) + float(tile * 128)
        hot[tile * 128:(tile + 1) * 128, :] = jnp.where(row == wanted, 1.0, 0.0).astype(jnp.bfloat16)

    def z_arrival(b, k, from_left):
        z_copy(b, k, zr_send, right).wait_recv()
        if from_left:
            @pl.when(has_right)
            def _():
                z_copy(b, k, zr_send, right).start()
        else:
            @pl.when(has_left)
            def _():
                z_copy(b, k, zl_send, left).start()

        @pl.when(k < 5)
        def _():
            y_copy(b, k, z_chunk(k), w).start()

        @pl.when(k < 2)
        def _():
            x_copy(b, k, z_chunk(k), w).start()

    def relay(tick):
        t = tick // 6 + 1
        k = tick % 6

        @pl.when(jnp.logical_and(t < line, zz - t >= 0))
        def _():
            z_arrival(zz - t, k, True)

        @pl.when(jnp.logical_and(t < line, zz + t < line))
        def _():
            z_arrival(zz + t, k, False)

        q = tick - 1

        @pl.when(jnp.logical_and(q >= 0, q < 4))
        def _():
            y_copy(zz, q, own_chunk(q), 1 - w).wait_recv()
            x_copy(zz, q, own_chunk(q), 1 - w).start()

        @pl.when(jnp.logical_and(q >= 4, q < 4 + 5 * (line - 1)))
        def _():
            b = block_of((q - 4) // 5 + 1)
            k = (q - 4) % 5
            y_copy(b, k, z_chunk(k), 1 - w).wait_recv()

            @pl.when(k < 3)
            def _():
                x_copy(b, k + 2, z_chunk(k), 1 - w).start()

    def window_of(n):
        return pl.ds(pl.multiple_of(n * window, window), window)

    def terms(blocks, n, picked):
        value = None
        for c in picked:
            queries = [held[b, c].reshape(2 * rows, chunk) for b in blocks]
            term = product(jnp.concatenate(queries, axis=0), stored[c, window_of(n), :], across)
            value = term if value is None else value + term
        return [value[i * 2 * rows:(i + 1) * 2 * rows] for i in range(len(blocks))]

    def whole(blocks, n):
        for b, value in zip(blocks, terms(blocks, n, range(chunks))):
            acc[b, :, window_of(n)] = value

    def x_arrivals(b, first, last):
        for k in range(first, last):
            x_copy(b, k, 0, w).wait_recv()

    def all_x_arrivals(b):
        x_arrivals(b, 0, 4)

        @pl.when(b != zz)
        def _():
            x_arrivals(b, 4, 5)

    def finish(b):
        c_copy(b).wait_recv()
        both = jnp.concatenate(split(acc[b] + arrived[b]), axis=0)
        value = product(both, hot[...])
        total[b] = value[:2 * rows] + value[2 * rows:]
        out_copy(b).start()

    alone = 6 * (line - 2) + 4

    def compute(tick):
        p = (tick - 12) // 12
        n = (tick - 12) % 12

        @pl.when(jnp.logical_and(tick >= 12, jnp.logical_and(n < slices, p < line // 2 - 1)))
        def _():
            one = jnp.where(p == 0, zz, block_of(2 * p))
            other = block_of(2 * p + 1)

            @pl.when(n == 0)
            def _():
                @pl.when(p == 0)
                def _():
                    pltpu.make_async_copy(stored, stored, load_sem).wait()

                all_x_arrivals(one)
                all_x_arrivals(other)

            whole([one, other], n)

            @pl.when(n == slices - 1)
            def _():
                c_copy(one).start()
                c_copy(other).start()

        @pl.when(jnp.logical_and(tick >= alone, tick < alone + slices))
        def _():
            b = block_of(line - 2)

            @pl.when(tick == alone)
            def _():
                all_x_arrivals(b)

            whole([b], tick - alone)

            @pl.when(tick == alone + slices - 1)
            def _():
                c_copy(b).start()

    ticks = max(6 * (line - 1), 5 * line, alone + slices)

    @pl.loop(0, ticks)
    def _(tick):
        relay(tick)
        compute(tick)

    last = block_of(line - 1)
    mine = (2 * side, 2 * side + 1, 4 + side, 6, 7)
    pair = (2 - 2 * side, 3 - 2 * side)
    single = (5 - side,)

    def add(picked):
        @pl.loop(0, slices)
        def _(n):
            (value,) = terms([last], n, picked)
            acc[last, :, window_of(n)] = acc[last, :, window_of(n)] + value

    @pl.loop(0, slices)
    def _(n):
        (value,) = terms([last], n, mine)
        acc[last, :, window_of(n)] = value

    @pl.loop(0, line)
    def _(b):
        @pl.when(b != last)
        def _():
            finish(b)

    x_arrivals(last, 0, 4)
    add(pair)
    x_arrivals(last, 4, 5)
    add(single)
    c_copy(last).start()
    finish(last)

    def sent(b, count, send):
        span = held.at[b, pl.ds(0, count), w]
        remote(span, span, send.at[b], z_recv.at[b, 0], across_y).wait_send()

    @pl.loop(0, line)
    def _(b):
        @pl.when(jnp.logical_and(has_right, b <= zz))
        def _():
            sent(b, 6, zr_send)

        @pl.when(jnp.logical_and(has_left, b >= zz))
        def _():
            sent(b, 6, zl_send)

        @pl.when(b == zz)
        def _():
            sent(b, 4, y_send)
            sent(b, 4, x_send)

        @pl.when(b != zz)
        def _():
            sent(b, 5, y_send)
            sent(b, 5, x_send)

        c_copy(b).wait_send()
        out_copy(b).wait()


def scores_of(queries, basis_s, basis_a, eigvals, ids, train, devices):
    rows = queries.shape[0]
    chunk = queries.shape[1] // chunks
    rank = basis_s.shape[0]
    examples = train.shape[0]
    line = devices // 2
    dma = pltpu.SemaphoreType.DMA
    vmem = pl.BlockSpec(memory_space=pltpu.VMEM)
    return pl.pallas_call(
        functools.partial(score_kernel, line),
        out_shape=jax.ShapeDtypeStruct((line, 2 * rows, examples // 2), jnp.float32),
        in_specs=[vmem] * 5 + [pl.BlockSpec(memory_space=pl.ANY)],
        out_specs=pl.BlockSpec(memory_space=pl.ANY),
        scratch_shapes=[
            pltpu.VMEM((rank // 2 * rows, 2 * rank), jnp.float32),
            pltpu.VMEM((3 * rank // 2, rows * 2 * rank), jnp.bfloat16),
            pltpu.VMEM((chunks, examples, chunk), jnp.bfloat16),
            pltpu.VMEM((examples, examples // 2), jnp.bfloat16),
            pltpu.VMEM((line, chunks, 2, rows, chunk), jnp.bfloat16),
            pltpu.VMEM((line, 2 * rows, examples), jnp.float32),
            pltpu.VMEM((line, 2 * rows, examples), jnp.float32),
            pltpu.VMEM((line, 2 * rows, examples // 2), jnp.float32),
            dma,
            dma((line, 6)),
            dma((line, 5)),
            dma((line, 5)),
            *[dma((line,)) for _ in range(7)],
        ],
        compiler_params=pltpu.CompilerParams(
            collective_id=0, has_side_effects=True, vmem_limit_bytes=56 * 1024 * 1024
        ),
    )(queries, basis_s, basis_a, eigvals, ids, train)


def shards(devices, queries, basis_s, basis_a, eigvals, train_grads, example_ids):
    scores = scores_of(
        queries.reshape(queries.shape[0], -1), basis_s[0], basis_a[0], eigvals[0],
        example_ids, train_grads.reshape(train_grads.shape[0], -1), devices,
    )
    return scores.reshape(devices * queries.shape[0], -1)


def solution(mesh):
    return jax.shard_map(
        functools.partial(shards, mesh.shape["ex"]),
        mesh=mesh,
        in_specs=(
            P("ex", "lay", None),
            P("lay", None, None),
            P("lay", None, None),
            P("lay", None, None),
            P(("grp", "ex"), "lay", None),
            P(("grp", "ex"), None),
        ),
        out_specs=P(None, ("grp", "ex", "lay")),
        check_vma=False,
    )
```

```python
import functools

import jax
import jax.numpy as jnp
from jax import lax
from jax.experimental import pallas as pl
from jax.experimental.pallas import tpu as pltpu
from jax.sharding import PartitionSpec as P

damp_ratio = 0.1
chunks = 8
slices = 4
MESH = pl.DeviceIdType.MESH


def split(value):
    top = value.astype(jnp.bfloat16)
    return top, (value - top.astype(jnp.float32)).astype(jnp.bfloat16)


def ones_where(mask):
    return jnp.where(mask, 1.0, 0.0).astype(jnp.bfloat16)


def picks(shape, rule):
    return ones_where(rule(lax.broadcasted_iota(jnp.int32, shape, 0), lax.broadcasted_iota(jnp.int32, shape, 1)))


def product(a, b, dims=((1,), (0,))):
    return lax.dot_general(a, b, (dims, ((), ())), preferred_element_type=jnp.float32)


across = ((1,), (1,))


def twice_diagonal(part, rank):
    spread = product(part, picks((rank, 2 * rank), lambda r, c: r == c % rank))
    both = jnp.concatenate([spread, spread], axis=0)
    shape = (2 * rank, 2 * rank)
    same = lax.broadcasted_iota(jnp.int32, shape, 0) // rank == lax.broadcasted_iota(jnp.int32, shape, 1) // rank
    return jnp.where(same, both, 0.0).astype(jnp.bfloat16)


def rotate(queries_ref, s_ref, a_ref, eig_ref, turned, stacked):
    rows = queries_ref.shape[0]
    rank = s_ref.shape[0]
    half = rank // 2
    lane = 2 * rank
    a_top, a_low = (twice_diagonal(part, rank) for part in split(a_ref[...]))
    a_both = jnp.concatenate([a_top, a_low], axis=0)
    for i in range(half):
        tile = queries_ref[:, i * lane:(i + 1) * lane]
        turned[i * rows:(i + 1) * rows, :] = product(jnp.concatenate([tile, tile], axis=1), a_both)

    eye = picks((rank, rank), lambda r, c: r == c)
    s_parts = split(s_ref[...])
    forward = []
    back = []
    for top_or_low, part in enumerate(s_parts):
        flipped = product(eye, part, across).astype(jnp.bfloat16)
        sorted_rows = product(picks((rank, rank), lambda r, c: c == (r % half) * 2 + r // half), part).astype(jnp.bfloat16)

        def wanted(c):
            third = c // half
            return third < 2 if top_or_low == 0 else third == 2

        forward.append([
            product(flipped, picks((rank, 3 * half), lambda r, c: (r == 2 * (c % half) + b) & wanted(c)))
            for b in range(2)
        ])
        back.append([
            product(sorted_rows, picks((rank, 3 * half), lambda r, c: (r == c % half + b * half) & wanted(c)))
            for b in range(2)
        ])
    lhs_forward = jnp.concatenate([forward[0][b] + forward[1][b] for b in range(2)], axis=0).astype(jnp.bfloat16)
    lhs_back = jnp.concatenate([back[0][b] + back[1][b] for b in range(2)], axis=0).astype(jnp.bfloat16)

    eig = eig_ref[...]
    damping = damp_ratio * jnp.mean(eig)
    inverse = 1.0 / (jnp.concatenate([eig[:half], eig[half:]], axis=1) + damping)
    first = lax.broadcasted_iota(jnp.int32, (half, lane), 1) < rank

    def gather_halves(value):
        kept = jnp.where(first, value[:half], value[3 * half:])
        crossed = jnp.where(first, value[half:2 * half], value[2 * half:3 * half])
        return kept + pltpu.roll(crossed, rank, 1)

    def stack(at, value):
        top, low = split(value)
        stacked[0:half, at] = top
        stacked[half:2 * half, at] = low
        stacked[2 * half:3 * half, at] = top

    group = 8
    for base in range(0, rows, group):
        for n in range(base, base + group):
            stack(slice(n * lane, (n + 1) * lane), turned[pl.ds(n, half, stride=rows), :])
    for base in range(0, rows, group):
        span = slice(base * lane, (base + group) * lane)
        value = product(lhs_forward, stacked[:, span])
        for n in range(group):
            scaled = gather_halves(value[:, n * lane:(n + 1) * lane]) * inverse
            stack(slice((base + n) * lane, (base + n + 1) * lane), scaled)
    for base in range(0, rows, group):
        span = slice(base * lane, (base + group) * lane)
        value = product(lhs_back, stacked[:, span])
        for n in range(group):
            turned[pl.ds(base + n, half, stride=rows), :] = gather_halves(value[:, n * lane:(n + 1) * lane])
    return jnp.concatenate([a_top, a_top, a_low], axis=1)


def condition_chunk(turned, c, rows, per_chunk, a_all, write):
    lane = turned.shape[1]
    top, low = split(turned[pl.ds(pl.multiple_of(c * per_chunk * rows, 8), per_chunk * rows), :])
    value = product(jnp.concatenate([top, low, top], axis=1), a_all, across).astype(jnp.bfloat16)
    for i in range(per_chunk):
        write(slice(i * lane, (i + 1) * lane), value[i * rows:(i + 1) * rows])

def score_kernel(
    line, queries_ref, s_ref, a_ref, eig_ref, ids_ref, train_ref, total, acc, arrived, hot,
    turned, stacked, stored, held,
    load_sem, z_recv, y_recv, x_recv, zr_send, zl_send, y_send, x_send, c_recv, c_send,
):
    grp = lax.axis_index("grp")
    ex = lax.axis_index("ex")
    core = lax.axis_index("lay")
    zz = ex // 2
    w = ex % 2
    side = grp % 2
    rows = queries_ref.shape[0]
    examples = train_ref.shape[0]
    chunk = queries_ref.shape[1] // chunks
    half = examples // 2
    window = examples // slices
    right = {"ex": lax.rem(ex + 2, 2 * line)}
    left = {"ex": lax.rem(ex + 2 * line - 2, 2 * line)}
    across_y = {"ex": zz * 2 + (1 - w)}
    across_x = {"grp": (grp // 2) * 2 + (1 - side)}
    across_c = {"lay": 1 - core}
    has_left = zz > 0
    has_right = zz < line - 1
    lefts = zz
    rights = line - 1 - zz
    both_ways = jnp.minimum(lefts, rights)

    def z_chunk(k):
        return jnp.where(
            k < 2, 2 * side + k, jnp.where(k == 2, 4 + side, jnp.where(k < 5, 3 + k, 5 - side))
        )

    def own_chunk(k):
        return jnp.where(k < 2, 2 * side + k, jnp.where(k == 2, 4 + side, 6 + side))

    def remote(src, dst, send, recv, target):
        return pltpu.make_async_remote_copy(
            src_ref=src, dst_ref=dst, send_sem=send, recv_sem=recv,
            device_id=target, device_id_type=MESH,
        )

    def load(c):
        return pltpu.make_async_copy(
            train_ref.at[:, pl.ds(c * chunk, chunk)], stored.at[c], load_sem
        )

    def z_copy(b, k, send, target):
        slot = held.at[b, z_chunk(k), w]
        return remote(slot, slot, send.at[b], z_recv.at[b, k], target)

    def y_copy(b, k, c, column):
        slot = held.at[b, c, column]
        return remote(slot, slot, y_send.at[b], y_recv.at[b, k], across_y)

    def x_copy(b, k, c, column):
        slot = held.at[b, c, column]
        return remote(slot, slot, x_send.at[b], x_recv.at[b, k], across_x)

    def c_copy(b):
        return remote(acc.at[b], arrived.at[b], c_send.at[b], c_recv.at[b], across_c)

    def block_of(j):
        i = j - 1
        paired = i < 2 * both_ways
        t = jnp.where(paired, i // 2 + 1, j - both_ways)
        from_left = jnp.where(paired, jnp.asarray(i % 2 == 0).astype(jnp.int32), (lefts > rights).astype(jnp.int32))
        return jnp.where(from_left > 0, zz - t, zz + t)

    @pl.loop(0, chunks)
    def _(c):
        load(c).start()

    barrier = pltpu.get_barrier_semaphore()

    @pl.when(has_left)
    def _():
        pl.semaphore_signal(barrier, inc=1, device_id=left, device_id_type=MESH)

    @pl.when(has_right)
    def _():
        pl.semaphore_signal(barrier, inc=1, device_id=right, device_id_type=MESH)

    for target in (across_y, across_x, across_c):
        pl.semaphore_signal(barrier, inc=1, device_id=target, device_id_type=MESH)

    a_all = rotate(queries_ref, s_ref, a_ref, eig_ref, turned, stacked)

    def condition(c):
        def write(at, value):
            held[zz, c, w, :, at] = value

        condition_chunk(turned, c, rows, chunk // turned.shape[1], a_all, write)

    pl.semaphore_wait(barrier, 3 + has_left.astype(jnp.int32) + has_right.astype(jnp.int32))

    @pl.loop(0, 6)
    def _(k):
        condition(z_chunk(k))

        @pl.when(has_right)
        def _():
            z_copy(zz, k, zr_send, right).start()

        @pl.when(has_left)
        def _():
            z_copy(zz, k, zl_send, left).start()

        @pl.when(k < 3)
        def _():
            y_copy(zz, k, own_chunk(k), w).start()

        @pl.when(k == 4)
        def _():
            y_copy(zz, 3, own_chunk(3), w).start()

    @pl.loop(0, 2)
    def _(k):
        condition(2 - 2 * side + k)

    ids = ids_ref[...].astype(jnp.float32)
    wanted = jnp.where(core == 0, ids[:, :half], ids[:, half:])
    for tile in range(examples // 128):
        row = lax.broadcasted_iota(jnp.int32, (128, half), 0).astype(jnp.float32) + float(tile * 128)
        hot[tile * 128:(tile + 1) * 128, :] = jnp.where(row == wanted, 1.0, 0.0).astype(jnp.bfloat16)

    def z_arrival(b, k, from_left):
        z_copy(b, k, zr_send, right).wait_recv()
        if from_left:
            @pl.when(has_right)
            def _():
                z_copy(b, k, zr_send, right).start()
        else:
            @pl.when(has_left)
            def _():
                z_copy(b, k, zl_send, left).start()

        @pl.when(k < 5)
        def _():
            y_copy(b, k, z_chunk(k), w).start()

        @pl.when(k < 2)
        def _():
            x_copy(b, k, z_chunk(k), w).start()

    def relay(tick):
        t = tick // 6 + 1
        k = tick % 6

        @pl.when(jnp.logical_and(t < line, zz - t >= 0))
        def _():
            z_arrival(zz - t, k, True)

        @pl.when(jnp.logical_and(t < line, zz + t < line))
        def _():
            z_arrival(zz + t, k, False)

        q = tick - 1

        @pl.when(jnp.logical_and(q >= 0, q < 4))
        def _():
            y_copy(zz, q, own_chunk(q), 1 - w).wait_recv()
            x_copy(zz, q, own_chunk(q), 1 - w).start()

        @pl.when(jnp.logical_and(q >= 4, q < 4 + 5 * (line - 1)))
        def _():
            b = block_of((q - 4) // 5 + 1)
            k = (q - 4) % 5
            y_copy(b, k, z_chunk(k), 1 - w).wait_recv()

            @pl.when(k < 3)
            def _():
                x_copy(b, k + 2, z_chunk(k), 1 - w).start()

    def window_of(n):
        return pl.ds(pl.multiple_of(n * window, window), window)

    def terms(blocks, n, picked):
        value = None
        for c in picked:
            queries = [held[b, c].reshape(2 * rows, chunk) for b in blocks]
            term = product(jnp.concatenate(queries, axis=0), stored[c, window_of(n), :], across)
            value = term if value is None else value + term
        return [value[i * 2 * rows:(i + 1) * 2 * rows] for i in range(len(blocks))]

    def whole(blocks, n):
        for b, value in zip(blocks, terms(blocks, n, range(chunks))):
            acc[b, :, window_of(n)] = value

    def x_arrivals(b, first, last):
        for k in range(first, last):
            x_copy(b, k, 0, w).wait_recv()

    def all_x_arrivals(b):
        x_arrivals(b, 0, 4)

        @pl.when(b != zz)
        def _():
            x_arrivals(b, 4, 5)

    def finish(b):
        c_copy(b).wait_recv()
        both = jnp.concatenate(split(acc[b] + arrived[b]), axis=0)
        value = product(both, hot[...])
        total[b] = value[:2 * rows] + value[2 * rows:]

    alone = 6 * (line - 2) + 4

    def compute(tick):
        p = (tick - 12) // 12
        n = (tick - 12) % 12

        @pl.when(jnp.logical_and(tick >= 12, jnp.logical_and(n < slices, p < line // 2 - 1)))
        def _():
            one = jnp.where(p == 0, zz, block_of(2 * p))
            other = block_of(2 * p + 1)

            @pl.when(n == 0)
            def _():
                @pl.when(p == 0)
                def _():
                    pltpu.make_async_copy(stored, stored, load_sem).wait()

                all_x_arrivals(one)
                all_x_arrivals(other)

            whole([one, other], n)

            @pl.when(n == slices - 1)
            def _():
                c_copy(one).start()
                c_copy(other).start()

        @pl.when(jnp.logical_and(tick >= alone, tick < alone + slices))
        def _():
            b = block_of(line - 2)

            @pl.when(tick == alone)
            def _():
                all_x_arrivals(b)

            whole([b], tick - alone)

            @pl.when(tick == alone + slices - 1)
            def _():
                c_copy(b).start()

    ticks = max(6 * (line - 1), 5 * line, alone + slices)

    @pl.loop(0, ticks)
    def _(tick):
        relay(tick)
        compute(tick)

    last = block_of(line - 1)
    mine = (2 * side, 2 * side + 1, 4 + side, 6, 7)
    pair = (2 - 2 * side, 3 - 2 * side)
    single = (5 - side,)

    def add(picked):
        @pl.loop(0, slices)
        def _(n):
            (value,) = terms([last], n, picked)
            acc[last, :, window_of(n)] = acc[last, :, window_of(n)] + value

    @pl.loop(0, slices)
    def _(n):
        (value,) = terms([last], n, mine)
        acc[last, :, window_of(n)] = value

    @pl.loop(0, line)
    def _(b):
        @pl.when(b != last)
        def _():
            finish(b)

    x_arrivals(last, 0, 4)
    add(pair)
    x_arrivals(last, 4, 5)
    add(single)
    c_copy(last).start()
    c_copy(last).wait_recv()

    def sent(b, count, send):
        span = held.at[b, pl.ds(0, count), w]
        remote(span, span, send.at[b], z_recv.at[b, 0], across_y).wait_send()

    @pl.loop(0, line)
    def _(b):
        @pl.when(jnp.logical_and(has_right, b <= zz))
        def _():
            sent(b, 6, zr_send)

        @pl.when(jnp.logical_and(has_left, b >= zz))
        def _():
            sent(b, 6, zl_send)

        @pl.when(b == zz)
        def _():
            sent(b, 4, y_send)
            sent(b, 4, x_send)

        @pl.when(b != zz)
        def _():
            sent(b, 5, y_send)
            sent(b, 5, x_send)

        c_copy(b).wait_send()


def scores_of(queries, basis_s, basis_a, eigvals, ids, train, devices):
    rows = queries.shape[0]
    chunk = queries.shape[1] // chunks
    rank = basis_s.shape[0]
    examples = train.shape[0]
    line = devices // 2
    dma = pltpu.SemaphoreType.DMA
    vmem = pl.BlockSpec(memory_space=pltpu.VMEM)
    return pl.pallas_call(
        functools.partial(score_kernel, line),
        out_shape=[
            pltpu.VMEM((line, 2 * rows, examples // 2), jnp.float32),
            pltpu.VMEM((line, 2 * rows, examples), jnp.float32),
            pltpu.VMEM((line, 2 * rows, examples), jnp.float32),
            pltpu.VMEM((examples, examples // 2), jnp.bfloat16),
        ],
        in_specs=[vmem] * 5 + [pl.BlockSpec(memory_space=pltpu.HBM)],
        out_specs=[vmem] * 4,
        scratch_shapes=[
            pltpu.VMEM((rank // 2 * rows, 2 * rank), jnp.float32),
            pltpu.VMEM((3 * rank // 2, rows * 2 * rank), jnp.bfloat16),
            pltpu.VMEM((chunks, examples, chunk), jnp.bfloat16),
            pltpu.VMEM((line, chunks, 2, rows, chunk), jnp.bfloat16),
            dma,
            dma((line, 6)),
            dma((line, 5)),
            dma((line, 5)),
            *[dma((line,)) for _ in range(6)],
        ],
        compiler_params=pltpu.CompilerParams(
            collective_id=0, has_side_effects=True, vmem_limit_bytes=52 * 1024 * 1024
        ),
    )(queries, basis_s, basis_a, eigvals, ids, train)


def last_of(line):
    zz = lax.axis_index("ex") // 2
    return jnp.where(zz > line - 1 - zz, 0, line - 1)


def finish_kernel(line, total_ref, acc_ref, arrived_ref, hot_ref, out_ref, done, sems):
    zz = lax.axis_index("ex") // 2
    last = jnp.where(zz > line - 1 - zz, 0, line - 1)
    rows = total_ref.shape[1]

    def out_copy(b, source):
        return pltpu.make_async_copy(source, out_ref.at[b], sems.at[b])

    @pl.loop(0, line)
    def _(b):
        @pl.when(b != last)
        def _():
            out_copy(b, total_ref.at[b]).start()

    both = jnp.concatenate(split(acc_ref[last] + arrived_ref[last]), axis=0)
    value = product(both, hot_ref[...])
    done[...] = value[:rows] + value[rows:]
    out_copy(last, done).start()

    @pl.loop(0, line)
    def _(b):
        out_copy(b, done).wait()


def finished(total, acc, arrived, hot):
    line = total.shape[0]
    vmem = pl.BlockSpec(memory_space=pltpu.VMEM)
    return pl.pallas_call(
        functools.partial(finish_kernel, line),
        out_shape=jax.ShapeDtypeStruct(total.shape, jnp.float32),
        in_specs=[vmem] * 4,
        out_specs=pl.BlockSpec(memory_space=pl.ANY),
        scratch_shapes=[
            pltpu.VMEM(total.shape[1:], jnp.float32),
            pltpu.SemaphoreType.DMA((line,)),
        ],
        compiler_params=pltpu.CompilerParams(vmem_limit_bytes=8 * 1024 * 1024),
    )(total, acc, arrived, hot)


def shards(devices, queries, basis_s, basis_a, eigvals, train_grads, example_ids):
    parts = scores_of(
        queries.reshape(queries.shape[0], -1), basis_s[0], basis_a[0], eigvals[0],
        example_ids, train_grads.reshape(train_grads.shape[0], -1), devices,
    )
    return finished(*parts).reshape(devices * queries.shape[0], -1)


def solution(mesh):
    return jax.shard_map(
        functools.partial(shards, mesh.shape["ex"]),
        mesh=mesh,
        in_specs=(
            P("ex", "lay", None),
            P("lay", None, None),
            P("lay", None, None),
            P("lay", None, None),
            P(("grp", "ex"), "lay", None),
            P(("grp", "ex"), None),
        ),
        out_specs=P(None, ("grp", "ex", "lay")),
        check_vma=False,
    )
```

```python
import functools

import jax
import jax.numpy as jnp
from jax import lax
from jax.experimental import pallas as pl
from jax.experimental.pallas import tpu as pltpu
from jax.sharding import PartitionSpec as P

damp_ratio = 0.1
chunks = 8
slices = 4
late = 12
own_tick = 9
MESH = pl.DeviceIdType.MESH


def split(value):
    top = value.astype(jnp.bfloat16)
    return top, (value - top.astype(jnp.float32)).astype(jnp.bfloat16)


def ones_where(mask):
    return jnp.where(mask, 1.0, 0.0).astype(jnp.bfloat16)


def picks(shape, rule):
    return ones_where(rule(lax.broadcasted_iota(jnp.int32, shape, 0), lax.broadcasted_iota(jnp.int32, shape, 1)))


def product(a, b, dims=((1,), (0,))):
    return lax.dot_general(a, b, (dims, ((), ())), preferred_element_type=jnp.float32)


across = ((1,), (1,))


def twice_diagonal(part, rank):
    spread = product(part, picks((rank, 2 * rank), lambda r, c: r == c % rank))
    both = jnp.concatenate([spread, spread], axis=0)
    shape = (2 * rank, 2 * rank)
    same = lax.broadcasted_iota(jnp.int32, shape, 0) // rank == lax.broadcasted_iota(jnp.int32, shape, 1) // rank
    return jnp.where(same, both, 0.0).astype(jnp.bfloat16)


def rotate(queries_ref, s_ref, a_ref, eig_ref, turned, stacked):
    rows = queries_ref.shape[0]
    rank = s_ref.shape[0]
    half = rank // 2
    lane = 2 * rank
    a_top, a_low = (twice_diagonal(part, rank) for part in split(a_ref[...]))
    a_both = jnp.concatenate([a_top, a_low], axis=0)
    for i in range(half):
        tile = queries_ref[:, i * lane:(i + 1) * lane]
        turned[i * rows:(i + 1) * rows, :] = product(jnp.concatenate([tile, tile], axis=1), a_both)

    eye = picks((rank, rank), lambda r, c: r == c)
    s_parts = split(s_ref[...])
    forward = []
    back = []
    for top_or_low, part in enumerate(s_parts):
        flipped = product(eye, part, across).astype(jnp.bfloat16)
        sorted_rows = product(picks((rank, rank), lambda r, c: c == (r % half) * 2 + r // half), part).astype(jnp.bfloat16)

        def wanted(c):
            third = c // half
            return third < 2 if top_or_low == 0 else third == 2

        forward.append([
            product(flipped, picks((rank, 3 * half), lambda r, c: (r == 2 * (c % half) + b) & wanted(c)))
            for b in range(2)
        ])
        back.append([
            product(sorted_rows, picks((rank, 3 * half), lambda r, c: (r == c % half + b * half) & wanted(c)))
            for b in range(2)
        ])
    lhs_forward = jnp.concatenate([forward[0][b] + forward[1][b] for b in range(2)], axis=0).astype(jnp.bfloat16)
    lhs_back = jnp.concatenate([back[0][b] + back[1][b] for b in range(2)], axis=0).astype(jnp.bfloat16)

    eig = eig_ref[...]
    damping = damp_ratio * jnp.mean(eig)
    inverse = 1.0 / (jnp.concatenate([eig[:half], eig[half:]], axis=1) + damping)
    first = lax.broadcasted_iota(jnp.int32, (half, lane), 1) < rank

    def gather_halves(value):
        kept = jnp.where(first, value[:half], value[3 * half:])
        crossed = jnp.where(first, value[half:2 * half], value[2 * half:3 * half])
        return kept + pltpu.roll(crossed, rank, 1)

    def stack(at, value):
        top, low = split(value)
        stacked[0:half, at] = top
        stacked[half:2 * half, at] = low
        stacked[2 * half:3 * half, at] = top

    group = 8
    for base in range(0, rows, group):
        for n in range(base, base + group):
            stack(slice(n * lane, (n + 1) * lane), turned[pl.ds(n, half, stride=rows), :])
    for base in range(0, rows, group):
        span = slice(base * lane, (base + group) * lane)
        value = product(lhs_forward, stacked[:, span])
        for n in range(group):
            scaled = gather_halves(value[:, n * lane:(n + 1) * lane]) * inverse
            stack(slice((base + n) * lane, (base + n + 1) * lane), scaled)
    for base in range(0, rows, group):
        span = slice(base * lane, (base + group) * lane)
        value = product(lhs_back, stacked[:, span])
        for n in range(group):
            turned[pl.ds(base + n, half, stride=rows), :] = gather_halves(value[:, n * lane:(n + 1) * lane])
    return jnp.concatenate([a_top, a_top, a_low], axis=1)


def condition_chunk(turned, c, rows, per_chunk, a_all, write):
    lane = turned.shape[1]
    top, low = split(turned[pl.ds(pl.multiple_of(c * per_chunk * rows, 8), per_chunk * rows), :])
    value = product(jnp.concatenate([top, low, top], axis=1), a_all, across).astype(jnp.bfloat16)
    for i in range(per_chunk):
        write(slice(i * lane, (i + 1) * lane), value[i * rows:(i + 1) * rows])

def nth_block(j, zz, line):
    lefts = zz
    rights = line - 1 - zz
    both_ways = jnp.minimum(lefts, rights)
    i = j - 1
    paired = i < 2 * both_ways
    t = jnp.where(paired, i // 2 + 1, j - both_ways)
    from_left = jnp.where(paired, jnp.asarray(i % 2 == 0).astype(jnp.int32), (lefts > rights).astype(jnp.int32))
    return jnp.where(from_left > 0, zz - t, zz + t)


def score_kernel(
    line, queries_ref, s_ref, a_ref, eig_ref, ids_ref, train_ref, total, acc, arrived, hot,
    turned, stacked, stored, held,
    load_sem, z_recv, y_recv, x_recv, zr_send, zl_send, y_send, x_send, c_recv, c_send,
):
    grp = lax.axis_index("grp")
    ex = lax.axis_index("ex")
    core = lax.axis_index("lay")
    zz = ex // 2
    w = ex % 2
    side = grp % 2
    rows = queries_ref.shape[0]
    examples = train_ref.shape[0]
    chunk = queries_ref.shape[1] // chunks
    half = examples // 2
    window = examples // slices
    right = {"ex": lax.rem(ex + 2, 2 * line)}
    left = {"ex": lax.rem(ex + 2 * line - 2, 2 * line)}
    across_y = {"ex": zz * 2 + (1 - w)}
    across_x = {"grp": (grp // 2) * 2 + (1 - side)}
    across_c = {"lay": 1 - core}
    has_left = zz > 0
    has_right = zz < line - 1
    both_ways = jnp.minimum(zz, line - 1 - zz)

    def z_chunk(k):
        return jnp.where(
            k < 2, 2 * side + k, jnp.where(
                k == 2, 4 + side, jnp.where(k < 5, 3 + k, jnp.where(k == 5, 5 - side, 3 - 2 * side))
            )
        )

    def own_chunk(k):
        return jnp.where(k < 2, 2 * side + k, jnp.where(k == 2, 4 + side, 6 + side))

    def remote(src, dst, send, recv, target):
        return pltpu.make_async_remote_copy(
            src_ref=src, dst_ref=dst, send_sem=send, recv_sem=recv,
            device_id=target, device_id_type=MESH,
        )

    def load(c):
        return pltpu.make_async_copy(
            train_ref.at[:, pl.ds(c * chunk, chunk)], stored.at[c], load_sem
        )

    def z_copy(b, k, send, target):
        slot = held.at[b, z_chunk(k), w]
        return remote(slot, slot, send.at[b], z_recv.at[b, k], target)

    def y_copy(b, k, c, column):
        slot = held.at[b, c, column]
        return remote(slot, slot, y_send.at[b], y_recv.at[b, k], across_y)

    def x_copy(b, k, c, column):
        slot = held.at[b, c, column]
        return remote(slot, slot, x_send.at[b], x_recv.at[b, k], across_x)

    def c_copy(b):
        return remote(acc.at[b], arrived.at[b], c_send.at[b], c_recv.at[b], across_c)

    def block_of(j):
        return nth_block(j, zz, line)

    @pl.loop(0, chunks)
    def _(c):
        load(c).start()

    barrier = pltpu.get_barrier_semaphore()

    @pl.when(has_left)
    def _():
        pl.semaphore_signal(barrier, inc=1, device_id=left, device_id_type=MESH)

    @pl.when(has_right)
    def _():
        pl.semaphore_signal(barrier, inc=1, device_id=right, device_id_type=MESH)

    for target in (across_y, across_x, across_c):
        pl.semaphore_signal(barrier, inc=1, device_id=target, device_id_type=MESH)

    a_all = rotate(queries_ref, s_ref, a_ref, eig_ref, turned, stacked)

    def condition(c):
        def write(at, value):
            held[zz, c, w, :, at] = value

        condition_chunk(turned, c, rows, chunk // turned.shape[1], a_all, write)

    pl.semaphore_wait(barrier, 3 + has_left.astype(jnp.int32) + has_right.astype(jnp.int32))

    def send_z(k):
        @pl.when(has_right)
        def _():
            z_copy(zz, k, zr_send, right).start()

        @pl.when(has_left)
        def _():
            z_copy(zz, k, zl_send, left).start()

    @pl.loop(0, 6)
    def _(k):
        condition(z_chunk(k))
        send_z(k)

        @pl.when(k < 3)
        def _():
            y_copy(zz, k, own_chunk(k), w).start()

        @pl.when(k == 4)
        def _():
            y_copy(zz, 3, own_chunk(3), w).start()

    @pl.loop(0, 2)
    def _(k):
        condition(2 - 2 * side + k)

    ids = ids_ref[...].astype(jnp.float32)
    wanted = jnp.where(core == 0, ids[:, :half], ids[:, half:])
    for tile in range(examples // 128):
        row = lax.broadcasted_iota(jnp.int32, (128, half), 0).astype(jnp.float32) + float(tile * 128)
        hot[tile * 128:(tile + 1) * 128, :] = jnp.where(row == wanted, 1.0, 0.0).astype(jnp.bfloat16)

    def z_arrival(b, k, from_left, near):
        z_copy(b, k, zr_send, right).wait_recv()
        if from_left:
            @pl.when(has_right)
            def _():
                z_copy(b, k, zr_send, right).start()
        else:
            @pl.when(has_left)
            def _():
                z_copy(b, k, zl_send, left).start()

        @pl.when(k < 5)
        def _():
            y_copy(b, k, z_chunk(k), w).start()

        @pl.when(jnp.logical_or(k == 0, jnp.logical_and(k == 1, jnp.logical_not(near))))
        def _():
            x_copy(b, k, z_chunk(k), w).start()

    def y_arrival(r):
        shared = r < 10 * both_ways
        t = r // 10 + 1
        near = jnp.where(r % 2 == 0, zz - t, zz + t)
        b = jnp.where(shared, near, block_of(r // 5 + 1))
        k = jnp.where(shared, r % 10 // 2, r % 5)
        y_copy(b, k, z_chunk(k), 1 - w).wait_recv()

        @pl.when(k < 3)
        def _():
            x_copy(b, k + 2, z_chunk(k), 1 - w).start()

    def relay(tick):
        t = tick // 6 + 1
        k = tick % 6

        @pl.when(jnp.logical_and(t < line, zz - t >= 0))
        def _():
            z_arrival(zz - t, k, True, t == 1)

        @pl.when(jnp.logical_and(t < line, zz + t < line))
        def _():
            z_arrival(zz + t, k, False, t == 1)

        @pl.when(jnp.asarray(tick) == late)
        def _():
            send_z(6)

        q = tick

        @pl.when(q < 4)
        def _():
            y_copy(zz, q, own_chunk(q), 1 - w).wait_recv()
            x_copy(zz, q, own_chunk(q), 1 - w).start()

        @pl.when(jnp.logical_and(q >= 4, q < 5 * line - 2))
        def _():
            y_arrival(q - 4)

    def window_of(n):
        return pl.ds(pl.multiple_of(n * window, window), window)

    def terms(blocks, n, picked):
        value = None
        for c in picked:
            queries = [held[b, c].reshape(2 * rows, chunk) for b in blocks]
            term = product(jnp.concatenate(queries, axis=0), stored[c, window_of(n), :], across)
            value = term if value is None else value + term
        return [value[i * 2 * rows:(i + 1) * 2 * rows] for i in range(len(blocks))]

    def put(blocks, n, picked, more=False):
        for b, value in zip(blocks, terms(blocks, n, picked)):
            acc[b, :, window_of(n)] = acc[b, :, window_of(n)] + value if more else value

    def last_arrivals(b):
        x_copy(b, 0, 0, w).wait_recv()
        for k in (2, 3):
            x_copy(b, k, 0, w).wait_recv()
        near = jnp.abs(b - zz) == 1

        @pl.when(near)
        def _():
            z_copy(b, 6, zr_send, right).wait_recv()

        @pl.when(jnp.logical_not(near))
        def _():
            x_copy(b, 1, 0, w).wait_recv()

        @pl.when(b != zz)
        def _():
            x_copy(b, 4, 0, w).wait_recv()

    def finish(b):
        c_copy(b).wait_recv()
        both = jnp.concatenate(split(acc[b] + arrived[b]), axis=0)
        value = product(both, hot[...])
        total[b] = value[:2 * rows] + value[2 * rows:]

    mine = (2 * side, 2 * side + 1, 4 + side, 6, 7)
    pair = (2 - 2 * side, 3 - 2 * side)
    single = (5 - side,)
    last = block_of(line - 1)
    ticks = max(6 * (line - 1), 5 * line - 2)

    def compute(tick):
        n = tick - own_tick

        @pl.when(jnp.logical_and(n >= 0, n < slices))
        def _():
            @pl.when(n == 0)
            def _():
                pltpu.make_async_copy(stored, stored, load_sem).wait()
                for k in range(4):
                    x_copy(zz, k, 0, w).wait_recv()

            put([zz], n, range(chunks))

            @pl.when(n == slices - 1)
            def _():
                c_copy(zz).start()

        @pl.when(tick == own_tick + 6)
        def _():
            finish(zz)

        p = (tick - 1) // 12
        step = (tick - 1) % 12
        one = block_of(2 * p - 1)
        other = block_of(2 * p)
        inside = jnp.logical_and(p >= 1, p < line // 2)

        @pl.when(jnp.logical_and(inside, step < 2))
        def _():
            @pl.loop(2 * step, 2 * step + 2)
            def _(m):
                put([one, other], m, mine)

        @pl.when(jnp.logical_and(inside, step == 3))
        def _():
            last_arrivals(one)
            last_arrivals(other)

            @pl.loop(0, slices)
            def _(m):
                put([one, other], m, pair + single, True)

            c_copy(one).start()
            c_copy(other).start()

        @pl.when(jnp.logical_and(inside, jnp.logical_and(step == 9, p < line // 2 - 1)))
        def _():
            finish(one)
            finish(other)

    @pl.loop(0, ticks)
    def _(tick):
        relay(tick)
        compute(tick)

    @pl.loop(0, slices)
    def _(m):
        put([last], m, mine[:4])

    y_arrival(5 * line - 6)

    for k in range(4):
        x_copy(last, k, 0, w).wait_recv()

    @pl.loop(0, slices)
    def _(m):
        put([last], m, mine[4:] + pair, True)

    x_copy(last, 4, 0, w).wait_recv()

    @pl.loop(0, slices)
    def _(m):
        put([last], m, single, True)

    for j in (line - 3, line - 2):
        c_copy(block_of(j)).wait_recv()

    c_copy(last).start()
    c_copy(last).wait_recv()

    def sent(b, count, send):
        span = held.at[b, pl.ds(0, count), w]
        remote(span, span, send.at[b], z_recv.at[b, 0], across_y).wait_send()

    @pl.loop(0, line)
    def _(b):
        @pl.when(jnp.logical_and(has_right, b < zz))
        def _():
            sent(b, 6, zr_send)

        @pl.when(jnp.logical_and(has_left, b > zz))
        def _():
            sent(b, 6, zl_send)

        @pl.when(b == zz)
        def _():
            @pl.when(has_right)
            def _():
                sent(b, 7, zr_send)

            @pl.when(has_left)
            def _():
                sent(b, 7, zl_send)

            sent(b, 4, y_send)
            sent(b, 4, x_send)

        @pl.when(b != zz)
        def _():
            sent(b, 5, y_send)

            @pl.when(jnp.abs(b - zz) == 1)
            def _():
                sent(b, 4, x_send)

            @pl.when(jnp.abs(b - zz) != 1)
            def _():
                sent(b, 5, x_send)

        c_copy(b).wait_send()


def scores_of(queries, basis_s, basis_a, eigvals, ids, train, devices):
    rows = queries.shape[0]
    chunk = queries.shape[1] // chunks
    rank = basis_s.shape[0]
    examples = train.shape[0]
    line = devices // 2
    dma = pltpu.SemaphoreType.DMA
    vmem = pl.BlockSpec(memory_space=pltpu.VMEM)
    return pl.pallas_call(
        functools.partial(score_kernel, line),
        out_shape=[
            pltpu.VMEM((line, 2 * rows, examples // 2), jnp.float32),
            pltpu.VMEM((line, 2 * rows, examples), jnp.float32),
            pltpu.VMEM((line, 2 * rows, examples), jnp.float32),
            pltpu.VMEM((examples, examples // 2), jnp.bfloat16),
        ],
        in_specs=[vmem] * 5 + [pl.BlockSpec(memory_space=pltpu.HBM)],
        out_specs=[vmem] * 4,
        scratch_shapes=[
            pltpu.VMEM((rank // 2 * rows, 2 * rank), jnp.float32),
            pltpu.VMEM((3 * rank // 2, rows * 2 * rank), jnp.bfloat16),
            pltpu.VMEM((chunks, examples, chunk), jnp.bfloat16),
            pltpu.VMEM((line, chunks, 2, rows, chunk), jnp.bfloat16),
            dma,
            dma((line, 7)),
            dma((line, 5)),
            dma((line, 5)),
            *[dma((line,)) for _ in range(6)],
        ],
        compiler_params=pltpu.CompilerParams(
            collective_id=0, has_side_effects=True, vmem_limit_bytes=52 * 1024 * 1024
        ),
    )(queries, basis_s, basis_a, eigvals, ids, train)


def finish_kernel(line, total_ref, acc_ref, arrived_ref, hot_ref, out_ref, done, sems):
    zz = lax.axis_index("ex") // 2
    rows = total_ref.shape[1]
    open_blocks = [nth_block(j, zz, line) for j in (line - 3, line - 2, line - 1)]

    def out_copy(b, source):
        return pltpu.make_async_copy(source, out_ref.at[b], sems.at[b])

    @pl.loop(0, line)
    def _(b):
        ready = jnp.logical_and(b != open_blocks[0], jnp.logical_and(b != open_blocks[1], b != open_blocks[2]))

        @pl.when(ready)
        def _():
            out_copy(b, total_ref.at[b]).start()

    for base, group in ((0, open_blocks[:2]), (2, open_blocks[2:])):
        both = jnp.concatenate([acc_ref[b] + arrived_ref[b] for b in group], axis=0)
        value = product(jnp.concatenate(split(both), axis=0), hot_ref[...])
        half = both.shape[0]
        value = value[:half] + value[half:]
        for i, b in enumerate(group):
            done[base + i] = value[i * rows:(i + 1) * rows]
            out_copy(b, done.at[base + i]).start()

    @pl.loop(0, line)
    def _(b):
        out_copy(b, done.at[0]).wait()


def finished(total, acc, arrived, hot):
    line = total.shape[0]
    vmem = pl.BlockSpec(memory_space=pltpu.VMEM)
    return pl.pallas_call(
        functools.partial(finish_kernel, line),
        out_shape=jax.ShapeDtypeStruct(total.shape, jnp.float32),
        in_specs=[vmem] * 4,
        out_specs=pl.BlockSpec(memory_space=pl.ANY),
        scratch_shapes=[
            pltpu.VMEM((3, *total.shape[1:]), jnp.float32),
            pltpu.SemaphoreType.DMA((line,)),
        ],
        compiler_params=pltpu.CompilerParams(vmem_limit_bytes=8 * 1024 * 1024),
    )(total, acc, arrived, hot)


def shards(devices, queries, basis_s, basis_a, eigvals, train_grads, example_ids):
    parts = scores_of(
        queries.reshape(queries.shape[0], -1), basis_s[0], basis_a[0], eigvals[0],
        example_ids, train_grads.reshape(train_grads.shape[0], -1), devices,
    )
    return finished(*parts).reshape(devices * queries.shape[0], -1)


def solution(mesh):
    return jax.shard_map(
        functools.partial(shards, mesh.shape["ex"]),
        mesh=mesh,
        in_specs=(
            P("ex", "lay", None),
            P("lay", None, None),
            P("lay", None, None),
            P("lay", None, None),
            P(("grp", "ex"), "lay", None),
            P(("grp", "ex"), None),
        ),
        out_specs=P(None, ("grp", "ex", "lay")),
        check_vma=False,
    )
```

```python
import functools

import jax
import jax.numpy as jnp
from jax import lax
from jax.experimental import pallas as pl
from jax.experimental.pallas import tpu as pltpu
from jax.sharding import PartitionSpec as P

damp_ratio = 0.1
chunks = 8
slices = 2
edge = 256
late = 12
own_tick = 9
MESH = pl.DeviceIdType.MESH


def split(value):
    top = value.astype(jnp.bfloat16)
    return top, (value - top.astype(jnp.float32)).astype(jnp.bfloat16)


def ones_where(mask):
    return jnp.where(mask, 1.0, 0.0).astype(jnp.bfloat16)


def picks(shape, rule):
    return ones_where(rule(lax.broadcasted_iota(jnp.int32, shape, 0), lax.broadcasted_iota(jnp.int32, shape, 1)))


def product(a, b, dims=((1,), (0,))):
    return lax.dot_general(a, b, (dims, ((), ())), preferred_element_type=jnp.float32)


across = ((1,), (1,))


def twice_diagonal(part, rank):
    spread = product(part, picks((rank, 2 * rank), lambda r, c: r == c % rank))
    both = jnp.concatenate([spread, spread], axis=0)
    shape = (2 * rank, 2 * rank)
    same = lax.broadcasted_iota(jnp.int32, shape, 0) // rank == lax.broadcasted_iota(jnp.int32, shape, 1) // rank
    return jnp.where(same, both, 0.0).astype(jnp.bfloat16)


def rotate(queries_ref, s_ref, a_ref, eig_ref, turned, stacked):
    rows = queries_ref.shape[0]
    rank = s_ref.shape[0]
    half = rank // 2
    lane = 2 * rank
    a_top, a_low = (twice_diagonal(part, rank) for part in split(a_ref[...]))
    a_both = jnp.concatenate([a_top, a_low], axis=0)
    for i in range(half):
        tile = queries_ref[:, i * lane:(i + 1) * lane]
        turned[i * rows:(i + 1) * rows, :] = product(jnp.concatenate([tile, tile], axis=1), a_both)

    eye = picks((rank, rank), lambda r, c: r == c)
    s_parts = split(s_ref[...])
    forward = []
    back = []
    for top_or_low, part in enumerate(s_parts):
        flipped = product(eye, part, across).astype(jnp.bfloat16)
        sorted_rows = product(picks((rank, rank), lambda r, c: c == (r % half) * 2 + r // half), part).astype(jnp.bfloat16)

        def wanted(c):
            third = c // half
            return third < 2 if top_or_low == 0 else third == 2

        forward.append([
            product(flipped, picks((rank, 3 * half), lambda r, c: (r == 2 * (c % half) + b) & wanted(c)))
            for b in range(2)
        ])
        back.append([
            product(sorted_rows, picks((rank, 3 * half), lambda r, c: (r == c % half + b * half) & wanted(c)))
            for b in range(2)
        ])
    lhs_forward = jnp.concatenate([forward[0][b] + forward[1][b] for b in range(2)], axis=0).astype(jnp.bfloat16)
    lhs_back = jnp.concatenate([back[0][b] + back[1][b] for b in range(2)], axis=0).astype(jnp.bfloat16)

    eig = eig_ref[...]
    damping = damp_ratio * jnp.mean(eig)
    inverse = 1.0 / (jnp.concatenate([eig[:half], eig[half:]], axis=1) + damping)
    first = lax.broadcasted_iota(jnp.int32, (half, lane), 1) < rank

    def gather_halves(value):
        kept = jnp.where(first, value[:half], value[3 * half:])
        crossed = jnp.where(first, value[half:2 * half], value[2 * half:3 * half])
        return kept + pltpu.roll(crossed, rank, 1)

    def stack(at, value):
        top, low = split(value)
        stacked[0:half, at] = top
        stacked[half:2 * half, at] = low
        stacked[2 * half:3 * half, at] = top

    group = 8
    for base in range(0, rows, group):
        for n in range(base, base + group):
            stack(slice(n * lane, (n + 1) * lane), turned[pl.ds(n, half, stride=rows), :])
    for base in range(0, rows, group):
        span = slice(base * lane, (base + group) * lane)
        value = product(lhs_forward, stacked[:, span])
        for n in range(group):
            scaled = gather_halves(value[:, n * lane:(n + 1) * lane]) * inverse
            stack(slice((base + n) * lane, (base + n + 1) * lane), scaled)
    for base in range(0, rows, group):
        span = slice(base * lane, (base + group) * lane)
        value = product(lhs_back, stacked[:, span])
        for n in range(group):
            turned[pl.ds(base + n, half, stride=rows), :] = gather_halves(value[:, n * lane:(n + 1) * lane])
    return jnp.concatenate([a_top, a_top, a_low], axis=1)


def condition_chunk(turned, c, rows, per_chunk, a_all, write):
    lane = turned.shape[1]
    top, low = split(turned[pl.ds(pl.multiple_of(c * per_chunk * rows, 8), per_chunk * rows), :])
    value = product(jnp.concatenate([top, low, top], axis=1), a_all, across).astype(jnp.bfloat16)
    for i in range(per_chunk):
        write(slice(i * lane, (i + 1) * lane), value[i * rows:(i + 1) * rows])

def nth_block(j, zz, line):
    lefts = zz
    rights = line - 1 - zz
    both_ways = jnp.minimum(lefts, rights)
    i = j - 1
    paired = i < 2 * both_ways
    t = jnp.where(paired, i // 2 + 1, j - both_ways)
    from_left = jnp.where(paired, jnp.asarray(i % 2 == 0).astype(jnp.int32), (lefts > rights).astype(jnp.int32))
    return jnp.where(from_left > 0, zz - t, zz + t)


def score_kernel(
    line, queries_ref, s_ref, a_ref, eig_ref, ids_ref, train_ref, total, acc, arrived, hot,
    turned, stacked, stored, turned_train, held,
    load_sem, z_recv, y_recv, x_recv, zr_send, zl_send, y_send, x_send, c_recv, c_send,
):
    grp = lax.axis_index("grp")
    ex = lax.axis_index("ex")
    core = lax.axis_index("lay")
    zz = ex // 2
    w = ex % 2
    side = grp % 2
    rows = queries_ref.shape[0]
    examples = train_ref.shape[0]
    chunk = queries_ref.shape[1] // chunks
    half = examples // 2
    window = examples // slices
    right = {"ex": lax.rem(ex + 2, 2 * line)}
    left = {"ex": lax.rem(ex + 2 * line - 2, 2 * line)}
    across_y = {"ex": zz * 2 + (1 - w)}
    across_x = {"grp": (grp // 2) * 2 + (1 - side)}
    across_c = {"lay": 1 - core}
    has_left = zz > 0
    has_right = zz < line - 1
    both_ways = jnp.minimum(zz, line - 1 - zz)

    def z_chunk(k):
        return jnp.where(
            k < 2, 2 * side + k, jnp.where(
                k == 2, 4 + side, jnp.where(k < 5, 3 + k, jnp.where(k == 5, 5 - side, 3 - 2 * side))
            )
        )

    def own_chunk(k):
        return jnp.where(k < 2, 2 * side + k, jnp.where(k == 2, 4 + side, 6 + side))

    def remote(src, dst, send, recv, target):
        return pltpu.make_async_remote_copy(
            src_ref=src, dst_ref=dst, send_sem=send, recv_sem=recv,
            device_id=target, device_id_type=MESH,
        )

    def load(c):
        return pltpu.make_async_copy(
            train_ref.at[:, pl.ds(c * chunk, chunk)], stored.at[c], load_sem
        )

    def z_copy(b, k, send, target):
        slot = held.at[b, z_chunk(k), w]
        return remote(slot, slot, send.at[b], z_recv.at[b, k], target)

    def y_copy(b, k, c, column):
        slot = held.at[b, c, column]
        return remote(slot, slot, y_send.at[b], y_recv.at[b, k], across_y)

    def x_copy(b, k, c, column):
        slot = held.at[b, c, column]
        return remote(slot, slot, x_send.at[b], x_recv.at[b, k], across_x)

    def c_copy(b):
        return remote(acc.at[b], arrived.at[b], c_send.at[b], c_recv.at[b], across_c)

    def block_of(j):
        return nth_block(j, zz, line)

    @pl.loop(0, chunks)
    def _(c):
        load(c).start()

    barrier = pltpu.get_barrier_semaphore()

    @pl.when(has_left)
    def _():
        pl.semaphore_signal(barrier, inc=1, device_id=left, device_id_type=MESH)

    @pl.when(has_right)
    def _():
        pl.semaphore_signal(barrier, inc=1, device_id=right, device_id_type=MESH)

    for target in (across_y, across_x, across_c):
        pl.semaphore_signal(barrier, inc=1, device_id=target, device_id_type=MESH)

    a_all = rotate(queries_ref, s_ref, a_ref, eig_ref, turned, stacked)

    def condition(c):
        def write(at, value):
            held[zz, c, w, :, at] = value

        condition_chunk(turned, c, rows, chunk // turned.shape[1], a_all, write)

    pl.semaphore_wait(barrier, 3 + has_left.astype(jnp.int32) + has_right.astype(jnp.int32))

    def send_z(k):
        @pl.when(has_right)
        def _():
            z_copy(zz, k, zr_send, right).start()

        @pl.when(has_left)
        def _():
            z_copy(zz, k, zl_send, left).start()

    @pl.loop(0, 6)
    def _(k):
        condition(z_chunk(k))
        send_z(k)

        @pl.when(k < 3)
        def _():
            y_copy(zz, k, own_chunk(k), w).start()

        @pl.when(k == 4)
        def _():
            y_copy(zz, 3, own_chunk(3), w).start()

    @pl.loop(0, 2)
    def _(k):
        condition(2 - 2 * side + k)

    ids = ids_ref[...].astype(jnp.float32)
    wanted = jnp.where(core == 0, ids[:, :half], ids[:, half:])
    for tile in range(examples // 128):
        row = lax.broadcasted_iota(jnp.int32, (128, half), 0).astype(jnp.float32) + float(tile * 128)
        hot[tile * 128:(tile + 1) * 128, :] = jnp.where(row == wanted, 1.0, 0.0).astype(jnp.bfloat16)

    def z_arrival(b, k, from_left, near):
        z_copy(b, k, zr_send, right).wait_recv()
        if from_left:
            @pl.when(has_right)
            def _():
                z_copy(b, k, zr_send, right).start()
        else:
            @pl.when(has_left)
            def _():
                z_copy(b, k, zl_send, left).start()

        @pl.when(k < 5)
        def _():
            y_copy(b, k, z_chunk(k), w).start()

        @pl.when(jnp.logical_or(k == 0, jnp.logical_and(k == 1, jnp.logical_not(near))))
        def _():
            x_copy(b, k, z_chunk(k), w).start()

    def y_arrival(r):
        shared = r < 10 * both_ways
        t = r // 10 + 1
        near = jnp.where(r % 2 == 0, zz - t, zz + t)
        b = jnp.where(shared, near, block_of(r // 5 + 1))
        k = jnp.where(shared, r % 10 // 2, r % 5)
        y_copy(b, k, z_chunk(k), 1 - w).wait_recv()

        @pl.when(k < 3)
        def _():
            x_copy(b, k + 2, z_chunk(k), 1 - w).start()

    def relay(tick):
        t = tick // 6 + 1
        k = tick % 6

        @pl.when(jnp.logical_and(t < line, zz - t >= 0))
        def _():
            z_arrival(zz - t, k, True, t == 1)

        @pl.when(jnp.logical_and(t < line, zz + t < line))
        def _():
            z_arrival(zz + t, k, False, t == 1)

        @pl.when(jnp.asarray(tick) == late)
        def _():
            send_z(6)

        q = tick

        @pl.when(q < 4)
        def _():
            y_copy(zz, q, own_chunk(q), 1 - w).wait_recv()
            x_copy(zz, q, own_chunk(q), 1 - w).start()

        @pl.when(jnp.logical_and(q >= 4, q < 5 * line - 2))
        def _():
            y_arrival(q - 4)

    def turn_train(c):
        eye = picks((edge, edge), lambda r, c: r == c)
        for at in range(0, chunk, edge):
            for n in range(slices):
                columns = slice(n * window, (n + 1) * window)
                turned_train[c, at:at + edge, columns] = product(
                    eye, stored[c, columns, at:at + edge], across
                ).astype(jnp.bfloat16)

    def put(blocks, n, picked, more=False):
        columns = slice(n * window, (n + 1) * window)
        value = None
        for c in picked:
            queries = [held[b, c].reshape(2 * rows, chunk) for b in blocks]
            term = product(jnp.concatenate(queries, axis=0), turned_train[c, :, columns])
            value = term if value is None else value + term
        for i, b in enumerate(blocks):
            part = value[i * 2 * rows:(i + 1) * 2 * rows]
            acc[b, :, columns] = acc[b, :, columns] + part if more else part

    def put_all(blocks, picked, more=False):
        for n in range(slices):
            put(blocks, n, picked, more)

    def last_arrivals(b):
        x_copy(b, 0, 0, w).wait_recv()
        for k in (2, 3):
            x_copy(b, k, 0, w).wait_recv()
        near = jnp.abs(b - zz) == 1

        @pl.when(near)
        def _():
            z_copy(b, 6, zr_send, right).wait_recv()

        @pl.when(jnp.logical_not(near))
        def _():
            x_copy(b, 1, 0, w).wait_recv()

        @pl.when(b != zz)
        def _():
            x_copy(b, 4, 0, w).wait_recv()

    def finish(b):
        c_copy(b).wait_recv()
        both = jnp.concatenate(split(acc[b] + arrived[b]), axis=0)
        value = product(both, hot[...])
        total[b] = value[:2 * rows] + value[2 * rows:]

    mine = (2 * side, 2 * side + 1, 4 + side, 6, 7)
    pair = (2 - 2 * side, 3 - 2 * side)
    single = (5 - side,)
    last = block_of(line - 1)
    ticks = max(6 * (line - 1), 5 * line - 2)

    def compute(tick):
        @pl.when(tick < chunks)
        def _():
            @pl.when(tick == 0)
            def _():
                pltpu.make_async_copy(stored, stored, load_sem).wait()

            turn_train(tick)

        for n in range(slices):
            @pl.when(tick == own_tick + n)
            def _():
                if n == 0:
                    for k in range(4):
                        x_copy(zz, k, 0, w).wait_recv()

                put([zz], n, range(chunks))

                if n == slices - 1:
                    c_copy(zz).start()

        @pl.when(tick == own_tick + 6)
        def _():
            finish(zz)

        p = (tick - 1) // 12
        step = (tick - 1) % 12
        one = block_of(2 * p - 1)
        other = block_of(2 * p)
        inside = jnp.logical_and(p >= 1, p < line // 2)

        for n in range(slices):
            @pl.when(jnp.logical_and(inside, step == n))
            def _():
                put([one, other], n, mine)

        @pl.when(jnp.logical_and(inside, step == 3))
        def _():
            last_arrivals(one)
            last_arrivals(other)

            put_all([one, other], pair + single, True)

            c_copy(one).start()
            c_copy(other).start()

        @pl.when(jnp.logical_and(inside, jnp.logical_and(step == 9, p < line // 2 - 1)))
        def _():
            finish(one)
            finish(other)

    @pl.loop(0, ticks)
    def _(tick):
        relay(tick)
        compute(tick)

    put_all([last], mine[:4])

    y_arrival(5 * line - 6)

    for k in range(4):
        x_copy(last, k, 0, w).wait_recv()

    put_all([last], mine[4:] + pair, True)

    x_copy(last, 4, 0, w).wait_recv()

    put_all([last], single, True)

    for j in (line - 3, line - 2):
        c_copy(block_of(j)).wait_recv()

    c_copy(last).start()
    c_copy(last).wait_recv()

    def sent(b, count, send):
        span = held.at[b, pl.ds(0, count), w]
        remote(span, span, send.at[b], z_recv.at[b, 0], across_y).wait_send()

    @pl.loop(0, line)
    def _(b):
        @pl.when(jnp.logical_and(has_right, b < zz))
        def _():
            sent(b, 6, zr_send)

        @pl.when(jnp.logical_and(has_left, b > zz))
        def _():
            sent(b, 6, zl_send)

        @pl.when(b == zz)
        def _():
            @pl.when(has_right)
            def _():
                sent(b, 7, zr_send)

            @pl.when(has_left)
            def _():
                sent(b, 7, zl_send)

            sent(b, 4, y_send)
            sent(b, 4, x_send)

        @pl.when(b != zz)
        def _():
            sent(b, 5, y_send)

            @pl.when(jnp.abs(b - zz) == 1)
            def _():
                sent(b, 4, x_send)

            @pl.when(jnp.abs(b - zz) != 1)
            def _():
                sent(b, 5, x_send)

        c_copy(b).wait_send()


def scores_of(queries, basis_s, basis_a, eigvals, ids, train, devices):
    rows = queries.shape[0]
    chunk = queries.shape[1] // chunks
    rank = basis_s.shape[0]
    examples = train.shape[0]
    line = devices // 2
    dma = pltpu.SemaphoreType.DMA
    vmem = pl.BlockSpec(memory_space=pltpu.VMEM)
    return pl.pallas_call(
        functools.partial(score_kernel, line),
        out_shape=[
            pltpu.VMEM((line, 2 * rows, examples // 2), jnp.float32),
            pltpu.VMEM((line, 2 * rows, examples), jnp.float32),
            pltpu.VMEM((line, 2 * rows, examples), jnp.float32),
            pltpu.VMEM((examples, examples // 2), jnp.bfloat16),
        ],
        in_specs=[vmem] * 5 + [pl.BlockSpec(memory_space=pltpu.HBM)],
        out_specs=[vmem] * 4,
        scratch_shapes=[
            pltpu.VMEM((rank // 2 * rows, 2 * rank), jnp.float32),
            pltpu.VMEM((3 * rank // 2, rows * 2 * rank), jnp.bfloat16),
            pltpu.VMEM((chunks, examples, chunk), jnp.bfloat16),
            pltpu.VMEM((chunks, chunk, examples), jnp.bfloat16),
            pltpu.VMEM((line, chunks, 2, rows, chunk), jnp.bfloat16),
            dma,
            dma((line, 7)),
            dma((line, 5)),
            dma((line, 5)),
            *[dma((line,)) for _ in range(6)],
        ],
        compiler_params=pltpu.CompilerParams(
            collective_id=0, has_side_effects=True, vmem_limit_bytes=52 * 1024 * 1024
        ),
    )(queries, basis_s, basis_a, eigvals, ids, train)


def finish_kernel(line, total_ref, acc_ref, arrived_ref, hot_ref, out_ref, done, sems):
    zz = lax.axis_index("ex") // 2
    rows = total_ref.shape[1]
    open_blocks = [nth_block(j, zz, line) for j in (line - 3, line - 2, line - 1)]

    def out_copy(b, source):
        return pltpu.make_async_copy(source, out_ref.at[b], sems.at[b])

    @pl.loop(0, line)
    def _(b):
        ready = jnp.logical_and(b != open_blocks[0], jnp.logical_and(b != open_blocks[1], b != open_blocks[2]))

        @pl.when(ready)
        def _():
            out_copy(b, total_ref.at[b]).start()

    for base, group in ((0, open_blocks[:2]), (2, open_blocks[2:])):
        both = jnp.concatenate([acc_ref[b] + arrived_ref[b] for b in group], axis=0)
        value = product(jnp.concatenate(split(both), axis=0), hot_ref[...])
        half = both.shape[0]
        value = value[:half] + value[half:]
        for i, b in enumerate(group):
            done[base + i] = value[i * rows:(i + 1) * rows]
            out_copy(b, done.at[base + i]).start()

    @pl.loop(0, line)
    def _(b):
        out_copy(b, done.at[0]).wait()


def finished(total, acc, arrived, hot):
    line = total.shape[0]
    vmem = pl.BlockSpec(memory_space=pltpu.VMEM)
    return pl.pallas_call(
        functools.partial(finish_kernel, line),
        out_shape=jax.ShapeDtypeStruct(total.shape, jnp.float32),
        in_specs=[vmem] * 4,
        out_specs=pl.BlockSpec(memory_space=pl.ANY),
        scratch_shapes=[
            pltpu.VMEM((3, *total.shape[1:]), jnp.float32),
            pltpu.SemaphoreType.DMA((line,)),
        ],
        compiler_params=pltpu.CompilerParams(vmem_limit_bytes=8 * 1024 * 1024),
    )(total, acc, arrived, hot)


def shards(devices, queries, basis_s, basis_a, eigvals, train_grads, example_ids):
    parts = scores_of(
        queries.reshape(queries.shape[0], -1), basis_s[0], basis_a[0], eigvals[0],
        example_ids, train_grads.reshape(train_grads.shape[0], -1), devices,
    )
    return finished(*parts).reshape(devices * queries.shape[0], -1)


def solution(mesh):
    return jax.shard_map(
        functools.partial(shards, mesh.shape["ex"]),
        mesh=mesh,
        in_specs=(
            P("ex", "lay", None),
            P("lay", None, None),
            P("lay", None, None),
            P("lay", None, None),
            P(("grp", "ex"), "lay", None),
            P(("grp", "ex"), None),
        ),
        out_specs=P(None, ("grp", "ex", "lay")),
        check_vma=False,
    )
```

```python
import functools

import jax
import jax.numpy as jnp
from jax import lax
from jax.experimental import pallas as pl
from jax.experimental.pallas import tpu as pltpu
from jax.sharding import PartitionSpec as P

damp_ratio = 0.1
chunks = 8
slices = 2
edge = 256
late = 12
own_tick = 9
MESH = pl.DeviceIdType.MESH


def split(value):
    top = value.astype(jnp.bfloat16)
    return top, (value - top.astype(jnp.float32)).astype(jnp.bfloat16)


def ones_where(mask):
    return jnp.where(mask, 1.0, 0.0).astype(jnp.bfloat16)


def picks(shape, rule):
    return ones_where(rule(lax.broadcasted_iota(jnp.int32, shape, 0), lax.broadcasted_iota(jnp.int32, shape, 1)))


def product(a, b, dims=((1,), (0,))):
    return lax.dot_general(a, b, (dims, ((), ())), preferred_element_type=jnp.float32)


across = ((1,), (1,))


def twice_diagonal(part, rank):
    spread = product(part, picks((rank, 2 * rank), lambda r, c: r == c % rank))
    both = jnp.concatenate([spread, spread], axis=0)
    shape = (2 * rank, 2 * rank)
    same = lax.broadcasted_iota(jnp.int32, shape, 0) // rank == lax.broadcasted_iota(jnp.int32, shape, 1) // rank
    return jnp.where(same, both, 0.0).astype(jnp.bfloat16)


def rotate(queries_ref, s_ref, a_ref, eig_ref, turned, stacked):
    rows = queries_ref.shape[0]
    rank = s_ref.shape[0]
    half = rank // 2
    lane = 2 * rank
    a_top, a_low = (twice_diagonal(part, rank) for part in split(a_ref[...]))
    a_both = jnp.concatenate([a_top, a_low], axis=0)
    for i in range(half):
        tile = queries_ref[:, i * lane:(i + 1) * lane]
        turned[i * rows:(i + 1) * rows, :] = product(jnp.concatenate([tile, tile], axis=1), a_both)

    eye = picks((rank, rank), lambda r, c: r == c)
    s_parts = split(s_ref[...])
    forward = []
    back = []
    for top_or_low, part in enumerate(s_parts):
        flipped = product(eye, part, across).astype(jnp.bfloat16)
        sorted_rows = product(picks((rank, rank), lambda r, c: c == (r % half) * 2 + r // half), part).astype(jnp.bfloat16)

        def wanted(c):
            third = c // half
            return third < 2 if top_or_low == 0 else third == 2

        forward.append([
            product(flipped, picks((rank, 3 * half), lambda r, c: (r == 2 * (c % half) + b) & wanted(c)))
            for b in range(2)
        ])
        back.append([
            product(sorted_rows, picks((rank, 3 * half), lambda r, c: (r == c % half + b * half) & wanted(c)))
            for b in range(2)
        ])
    lhs_forward = jnp.concatenate([forward[0][b] + forward[1][b] for b in range(2)], axis=0).astype(jnp.bfloat16)
    lhs_back = jnp.concatenate([back[0][b] + back[1][b] for b in range(2)], axis=0).astype(jnp.bfloat16)

    eig = eig_ref[...]
    damping = damp_ratio * jnp.mean(eig)
    inverse = 1.0 / (jnp.concatenate([eig[:half], eig[half:]], axis=1) + damping)
    first = lax.broadcasted_iota(jnp.int32, (half, lane), 1) < rank

    def gather_halves(value):
        kept = jnp.where(first, value[:half], value[3 * half:])
        crossed = jnp.where(first, value[half:2 * half], value[2 * half:3 * half])
        return kept + pltpu.roll(crossed, rank, 1)

    def stack(at, value):
        top, low = split(value)
        stacked[0:half, at] = top
        stacked[half:2 * half, at] = low
        stacked[2 * half:3 * half, at] = top

    group = 8
    for base in range(0, rows, group):
        for n in range(base, base + group):
            stack(slice(n * lane, (n + 1) * lane), turned[pl.ds(n, half, stride=rows), :])
    for base in range(0, rows, group):
        span = slice(base * lane, (base + group) * lane)
        value = product(lhs_forward, stacked[:, span])
        for n in range(group):
            scaled = gather_halves(value[:, n * lane:(n + 1) * lane]) * inverse
            stack(slice((base + n) * lane, (base + n + 1) * lane), scaled)
    for base in range(0, rows, group):
        span = slice(base * lane, (base + group) * lane)
        value = product(lhs_back, stacked[:, span])
        for n in range(group):
            turned[pl.ds(base + n, half, stride=rows), :] = gather_halves(value[:, n * lane:(n + 1) * lane])
    return jnp.concatenate([a_top, a_top, a_low], axis=1)


def condition_chunk(turned, c, rows, per_chunk, a_all, write):
    lane = turned.shape[1]
    top, low = split(turned[pl.ds(pl.multiple_of(c * per_chunk * rows, 8), per_chunk * rows), :])
    value = product(jnp.concatenate([top, low, top], axis=1), a_all, across).astype(jnp.bfloat16)
    for i in range(per_chunk):
        write(slice(i * lane, (i + 1) * lane), value[i * rows:(i + 1) * rows])

def nth_block(j, zz, line):
    lefts = zz
    rights = line - 1 - zz
    both_ways = jnp.minimum(lefts, rights)
    i = j - 1
    paired = i < 2 * both_ways
    t = jnp.where(paired, i // 2 + 1, j - both_ways)
    from_left = jnp.where(paired, jnp.asarray(i % 2 == 0).astype(jnp.int32), (lefts > rights).astype(jnp.int32))
    return jnp.where(from_left > 0, zz - t, zz + t)


def score_kernel(
    line, queries_ref, s_ref, a_ref, eig_ref, ids_ref, train_ref, total, acc, arrived, hot,
    turned, stacked, stored, turned_train, held,
    load_sem, z_recv, y_recv, x_recv, zr_send, zl_send, y_send, x_send, c_recv, c_send,
):
    grp = lax.axis_index("grp")
    ex = lax.axis_index("ex")
    core = lax.axis_index("lay")
    zz = ex // 2
    w = ex % 2
    side = grp % 2
    rows = queries_ref.shape[0]
    examples = train_ref.shape[0]
    chunk = queries_ref.shape[1] // chunks
    half = examples // 2
    window = examples // slices
    right = {"ex": lax.rem(ex + 2, 2 * line)}
    left = {"ex": lax.rem(ex + 2 * line - 2, 2 * line)}
    across_y = {"ex": zz * 2 + (1 - w)}
    across_x = {"grp": (grp // 2) * 2 + (1 - side)}
    across_c = {"lay": 1 - core}
    has_left = zz > 0
    has_right = zz < line - 1
    both_ways = jnp.minimum(zz, line - 1 - zz)

    def z_chunk(k):
        return jnp.where(
            k < 2, 2 * side + k, jnp.where(
                k == 2, 4 + side, jnp.where(k < 5, 3 + k, jnp.where(k == 5, 5 - side, 3 - 2 * side))
            )
        )

    def own_chunk(k):
        return jnp.where(k < 2, 2 * side + k, jnp.where(k == 2, 4 + side, 6 + side))

    def remote(src, dst, send, recv, target):
        return pltpu.make_async_remote_copy(
            src_ref=src, dst_ref=dst, send_sem=send, recv_sem=recv,
            device_id=target, device_id_type=MESH,
        )

    def load(c):
        return pltpu.make_async_copy(
            train_ref.at[:, pl.ds(c * chunk, chunk)], stored.at[c], load_sem
        )

    def z_copy(b, k, send, target):
        slot = held.at[b, z_chunk(k), w]
        return remote(slot, slot, send.at[b], z_recv.at[b, k], target)

    def y_copy(b, k, c, column):
        slot = held.at[b, c, column]
        return remote(slot, slot, y_send.at[b], y_recv.at[b, k], across_y)

    def x_copy(b, k, c, column):
        slot = held.at[b, c, column]
        return remote(slot, slot, x_send.at[b], x_recv.at[b, k], across_x)

    def c_copy(b):
        return remote(acc.at[b], arrived.at[b], c_send.at[b], c_recv.at[b], across_c)

    def block_of(j):
        return nth_block(j, zz, line)

    @pl.loop(0, chunks)
    def _(c):
        load(c).start()

    barrier = pltpu.get_barrier_semaphore()

    @pl.when(has_left)
    def _():
        pl.semaphore_signal(barrier, inc=1, device_id=left, device_id_type=MESH)

    @pl.when(has_right)
    def _():
        pl.semaphore_signal(barrier, inc=1, device_id=right, device_id_type=MESH)

    for target in (across_y, across_x, across_c):
        pl.semaphore_signal(barrier, inc=1, device_id=target, device_id_type=MESH)

    a_all = rotate(queries_ref, s_ref, a_ref, eig_ref, turned, stacked)

    def condition(c):
        def write(at, value):
            held[zz, c, w, :, at] = value

        condition_chunk(turned, c, rows, chunk // turned.shape[1], a_all, write)

    pl.semaphore_wait(barrier, 3 + has_left.astype(jnp.int32) + has_right.astype(jnp.int32))

    def send_z(k):
        @pl.when(has_right)
        def _():
            z_copy(zz, k, zr_send, right).start()

        @pl.when(has_left)
        def _():
            z_copy(zz, k, zl_send, left).start()

    @pl.loop(0, 6)
    def _(k):
        condition(z_chunk(k))
        send_z(k)

        @pl.when(k < 3)
        def _():
            y_copy(zz, k, own_chunk(k), w).start()

        @pl.when(k == 4)
        def _():
            y_copy(zz, 3, own_chunk(3), w).start()

    @pl.loop(0, 2)
    def _(k):
        condition(2 - 2 * side + k)

    ids = ids_ref[...].astype(jnp.float32)
    wanted = jnp.where(core == 0, ids[:, :half], ids[:, half:])
    for tile in range(examples // 128):
        row = lax.broadcasted_iota(jnp.int32, (128, half), 0).astype(jnp.float32) + float(tile * 128)
        hot[tile * 128:(tile + 1) * 128, :] = jnp.where(row == wanted, 1.0, 0.0).astype(jnp.bfloat16)

    def z_arrival(b, k, from_left, near):
        z_copy(b, k, zr_send, right).wait_recv()
        if from_left:
            @pl.when(has_right)
            def _():
                z_copy(b, k, zr_send, right).start()
        else:
            @pl.when(has_left)
            def _():
                z_copy(b, k, zl_send, left).start()

        @pl.when(k < 5)
        def _():
            y_copy(b, k, z_chunk(k), w).start()

        @pl.when(jnp.logical_or(k == 0, jnp.logical_and(k == 1, jnp.logical_not(near))))
        def _():
            x_copy(b, k, z_chunk(k), w).start()

    def y_arrival(r):
        shared = r < 10 * both_ways
        t = r // 10 + 1
        near = jnp.where(r % 2 == 0, zz - t, zz + t)
        b = jnp.where(shared, near, block_of(r // 5 + 1))
        k = jnp.where(shared, r % 10 // 2, r % 5)
        y_copy(b, k, z_chunk(k), 1 - w).wait_recv()

        @pl.when(k < 3)
        def _():
            x_copy(b, k + 2, z_chunk(k), 1 - w).start()

    def relay(tick):
        t = tick // 6 + 1
        k = tick % 6

        @pl.when(jnp.logical_and(t < line, zz - t >= 0))
        def _():
            z_arrival(zz - t, k, True, t == 1)

        @pl.when(jnp.logical_and(t < line, zz + t < line))
        def _():
            z_arrival(zz + t, k, False, t == 1)

        @pl.when(jnp.asarray(tick) == late)
        def _():
            send_z(6)

        q = tick

        @pl.when(q < 4)
        def _():
            y_copy(zz, q, own_chunk(q), 1 - w).wait_recv()
            x_copy(zz, q, own_chunk(q), 1 - w).start()

        @pl.when(jnp.logical_and(q >= 4, q < 5 * line - 2))
        def _():
            y_arrival(q - 4)

    def turn_train(c):
        eye = picks((edge, edge), lambda r, c: r == c)
        for at in range(0, chunk, edge):
            for n in range(slices):
                columns = slice(n * window, (n + 1) * window)
                turned_train[c, at:at + edge, columns] = product(
                    eye, stored[c, columns, at:at + edge], across
                ).astype(jnp.bfloat16)

    def put(blocks, n, picked, more=False):
        columns = slice(n * window, (n + 1) * window)
        value = None
        for c in picked:
            queries = [held[b, c].reshape(2 * rows, chunk) for b in blocks]
            term = product(jnp.concatenate(queries, axis=0), turned_train[c, :, columns])
            value = term if value is None else value + term
        for i, b in enumerate(blocks):
            part = value[i * 2 * rows:(i + 1) * 2 * rows]
            acc[b, :, columns] = acc[b, :, columns] + part if more else part

    def put_all(blocks, picked, more=False):
        for n in range(slices):
            put(blocks, n, picked, more)

    def last_arrivals(b):
        x_copy(b, 0, 0, w).wait_recv()
        for k in (2, 3):
            x_copy(b, k, 0, w).wait_recv()
        near = jnp.abs(b - zz) == 1

        @pl.when(near)
        def _():
            z_copy(b, 6, zr_send, right).wait_recv()

        @pl.when(jnp.logical_not(near))
        def _():
            x_copy(b, 1, 0, w).wait_recv()

        @pl.when(b != zz)
        def _():
            x_copy(b, 4, 0, w).wait_recv()

    def finish(blocks):
        for b in blocks:
            c_copy(b).wait_recv()
        both = jnp.concatenate([acc[b] + arrived[b] for b in blocks], axis=0)
        value = product(jnp.concatenate(split(both), axis=0), hot[...])
        value = value[:both.shape[0]] + value[both.shape[0]:]
        for i, b in enumerate(blocks):
            total[b] = value[i * 2 * rows:(i + 1) * 2 * rows]

    mine = (2 * side, 2 * side + 1, 4 + side, 6, 7)
    pair = (2 - 2 * side, 3 - 2 * side)
    single = (5 - side,)
    last = block_of(line - 1)
    ticks = max(6 * (line - 1), 5 * line - 2)

    def compute(tick):
        @pl.when(tick < chunks)
        def _():
            @pl.when(tick == 0)
            def _():
                pltpu.make_async_copy(stored, stored, load_sem).wait()

            turn_train(tick)

        for n in range(slices):
            @pl.when(tick == own_tick + n)
            def _():
                if n == 0:
                    for k in range(4):
                        x_copy(zz, k, 0, w).wait_recv()

                put([zz], n, range(chunks))

                if n == slices - 1:
                    c_copy(zz).start()

        @pl.when(tick == own_tick + 6)
        def _():
            finish([zz])

        p = (tick - 1) // 12
        step = (tick - 1) % 12
        one = block_of(2 * p - 1)
        other = block_of(2 * p)
        inside = jnp.logical_and(p >= 1, p < line // 2)

        for n in range(slices):
            @pl.when(jnp.logical_and(inside, step == n))
            def _():
                put([one, other], n, mine)

        @pl.when(jnp.logical_and(inside, step == 3))
        def _():
            last_arrivals(one)
            last_arrivals(other)

            put_all([one, other], pair + single, True)

            c_copy(one).start()
            c_copy(other).start()

        @pl.when(jnp.logical_and(inside, jnp.logical_and(step == 9, p < line // 2 - 1)))
        def _():
            finish([one, other])

    @pl.loop(0, ticks)
    def _(tick):
        relay(tick)
        compute(tick)

    put_all([last], mine[:4])

    y_arrival(5 * line - 6)

    for k in range(4):
        x_copy(last, k, 0, w).wait_recv()

    put_all([last], mine[4:] + pair, True)

    x_copy(last, 4, 0, w).wait_recv()

    def c_part(b, n):
        columns = slice(n * window, (n + 1) * window)
        return remote(acc.at[b, :, columns], arrived.at[b, :, columns], c_send.at[b], c_recv.at[b], across_c)

    for n in range(slices):
        put([last], n, single, True)
        c_part(last, n).start()

    finish([block_of(line - 3), block_of(line - 2)])
    c_copy(last).wait_recv()

    def sent(b, count, send):
        span = held.at[b, pl.ds(0, count), w]
        remote(span, span, send.at[b], z_recv.at[b, 0], across_y).wait_send()

    @pl.loop(0, line)
    def _(b):
        @pl.when(jnp.logical_and(has_right, b < zz))
        def _():
            sent(b, 6, zr_send)

        @pl.when(jnp.logical_and(has_left, b > zz))
        def _():
            sent(b, 6, zl_send)

        @pl.when(b == zz)
        def _():
            @pl.when(has_right)
            def _():
                sent(b, 7, zr_send)

            @pl.when(has_left)
            def _():
                sent(b, 7, zl_send)

            sent(b, 4, y_send)
            sent(b, 4, x_send)

        @pl.when(b != zz)
        def _():
            sent(b, 5, y_send)

            @pl.when(jnp.abs(b - zz) == 1)
            def _():
                sent(b, 4, x_send)

            @pl.when(jnp.abs(b - zz) != 1)
            def _():
                sent(b, 5, x_send)

        c_copy(b).wait_send()


def scores_of(queries, basis_s, basis_a, eigvals, ids, train, devices):
    rows = queries.shape[0]
    chunk = queries.shape[1] // chunks
    rank = basis_s.shape[0]
    examples = train.shape[0]
    line = devices // 2
    dma = pltpu.SemaphoreType.DMA
    vmem = pl.BlockSpec(memory_space=pltpu.VMEM)
    return pl.pallas_call(
        functools.partial(score_kernel, line),
        out_shape=[
            pltpu.VMEM((line, 2 * rows, examples // 2), jnp.float32),
            pltpu.VMEM((line, 2 * rows, examples), jnp.float32),
            pltpu.VMEM((line, 2 * rows, examples), jnp.float32),
            pltpu.VMEM((examples, examples // 2), jnp.bfloat16),
        ],
        in_specs=[vmem] * 5 + [pl.BlockSpec(memory_space=pltpu.HBM)],
        out_specs=[vmem] * 4,
        scratch_shapes=[
            pltpu.VMEM((rank // 2 * rows, 2 * rank), jnp.float32),
            pltpu.VMEM((3 * rank // 2, rows * 2 * rank), jnp.bfloat16),
            pltpu.VMEM((chunks, examples, chunk), jnp.bfloat16),
            pltpu.VMEM((chunks, chunk, examples), jnp.bfloat16),
            pltpu.VMEM((line, chunks, 2, rows, chunk), jnp.bfloat16),
            dma,
            dma((line, 7)),
            dma((line, 5)),
            dma((line, 5)),
            *[dma((line,)) for _ in range(6)],
        ],
        compiler_params=pltpu.CompilerParams(
            collective_id=0, has_side_effects=True, vmem_limit_bytes=52 * 1024 * 1024
        ),
    )(queries, basis_s, basis_a, eigvals, ids, train)


def finish_kernel(line, total_ref, acc_ref, arrived_ref, hot_ref, out_ref, done, sems):
    zz = lax.axis_index("ex") // 2
    rows = total_ref.shape[1]
    last = nth_block(line - 1, zz, line)

    def out_copy(b, source):
        return pltpu.make_async_copy(source, out_ref.at[b], sems.at[b])

    @pl.loop(0, line)
    def _(b):
        @pl.when(b != last)
        def _():
            out_copy(b, total_ref.at[b]).start()

    value = product(jnp.concatenate(split(acc_ref[last] + arrived_ref[last]), axis=0), hot_ref[...])
    done[...] = value[:rows] + value[rows:]
    out_copy(last, done).start()

    @pl.loop(0, line)
    def _(b):
        out_copy(b, done).wait()


def finished(total, acc, arrived, hot):
    line = total.shape[0]
    vmem = pl.BlockSpec(memory_space=pltpu.VMEM)
    return pl.pallas_call(
        functools.partial(finish_kernel, line),
        out_shape=jax.ShapeDtypeStruct(total.shape, jnp.float32),
        in_specs=[vmem] * 4,
        out_specs=pl.BlockSpec(memory_space=pl.ANY),
        scratch_shapes=[
            pltpu.VMEM(total.shape[1:], jnp.float32),
            pltpu.SemaphoreType.DMA((line,)),
        ],
        compiler_params=pltpu.CompilerParams(vmem_limit_bytes=8 * 1024 * 1024),
    )(total, acc, arrived, hot)


def shards(devices, queries, basis_s, basis_a, eigvals, train_grads, example_ids):
    parts = scores_of(
        queries.reshape(queries.shape[0], -1), basis_s[0], basis_a[0], eigvals[0],
        example_ids, train_grads.reshape(train_grads.shape[0], -1), devices,
    )
    return finished(*parts).reshape(devices * queries.shape[0], -1)


def solution(mesh):
    return jax.shard_map(
        functools.partial(shards, mesh.shape["ex"]),
        mesh=mesh,
        in_specs=(
            P("ex", "lay", None),
            P("lay", None, None),
            P("lay", None, None),
            P("lay", None, None),
            P(("grp", "ex"), "lay", None),
            P(("grp", "ex"), None),
        ),
        out_specs=P(None, ("grp", "ex", "lay")),
        check_vma=False,
    )
```

```python
import functools

import jax
import jax.numpy as jnp
from jax import lax
from jax.experimental import pallas as pl
from jax.experimental.pallas import tpu as pltpu
from jax.sharding import PartitionSpec as P

damp_ratio = 0.1
chunks = 8
slices = 2
edge = 256
late = 12
own_tick = 9
MESH = pl.DeviceIdType.MESH


def split(value):
    top = value.astype(jnp.bfloat16)
    return top, (value - top.astype(jnp.float32)).astype(jnp.bfloat16)


def ones_where(mask):
    return jnp.where(mask, 1.0, 0.0).astype(jnp.bfloat16)


def picks(shape, rule):
    return ones_where(rule(lax.broadcasted_iota(jnp.int32, shape, 0), lax.broadcasted_iota(jnp.int32, shape, 1)))


def product(a, b, dims=((1,), (0,))):
    return lax.dot_general(a, b, (dims, ((), ())), preferred_element_type=jnp.float32)


across = ((1,), (1,))


def twice_diagonal(part, rank):
    spread = product(part, picks((rank, 2 * rank), lambda r, c: r == c % rank))
    both = jnp.concatenate([spread, spread], axis=0)
    shape = (2 * rank, 2 * rank)
    same = lax.broadcasted_iota(jnp.int32, shape, 0) // rank == lax.broadcasted_iota(jnp.int32, shape, 1) // rank
    return jnp.where(same, both, 0.0).astype(jnp.bfloat16)


def rotate(queries_ref, s_ref, a_ref, eig_ref, turned, stacked):
    rows = queries_ref.shape[0]
    rank = s_ref.shape[0]
    half = rank // 2
    lane = 2 * rank
    a_top, a_low = (twice_diagonal(part, rank) for part in split(a_ref[...]))
    a_both = jnp.concatenate([a_top, a_low], axis=0)
    for i in range(half):
        tile = queries_ref[:, i * lane:(i + 1) * lane]
        turned[i * rows:(i + 1) * rows, :] = product(jnp.concatenate([tile, tile], axis=1), a_both)

    eye = picks((rank, rank), lambda r, c: r == c)
    s_parts = split(s_ref[...])
    forward = []
    back = []
    for top_or_low, part in enumerate(s_parts):
        flipped = product(eye, part, across).astype(jnp.bfloat16)
        sorted_rows = product(picks((rank, rank), lambda r, c: c == (r % half) * 2 + r // half), part).astype(jnp.bfloat16)

        def wanted(c):
            third = c // half
            return third < 2 if top_or_low == 0 else third == 2

        forward.append([
            product(flipped, picks((rank, 3 * half), lambda r, c: (r == 2 * (c % half) + b) & wanted(c)))
            for b in range(2)
        ])
        back.append([
            product(sorted_rows, picks((rank, 3 * half), lambda r, c: (r == c % half + b * half) & wanted(c)))
            for b in range(2)
        ])
    lhs_forward = jnp.concatenate([forward[0][b] + forward[1][b] for b in range(2)], axis=0).astype(jnp.bfloat16)
    lhs_back = jnp.concatenate([back[0][b] + back[1][b] for b in range(2)], axis=0).astype(jnp.bfloat16)

    eig = eig_ref[...]
    damping = damp_ratio * jnp.mean(eig)
    inverse = 1.0 / (jnp.concatenate([eig[:half], eig[half:]], axis=1) + damping)
    first = lax.broadcasted_iota(jnp.int32, (half, lane), 1) < rank

    def gather_halves(value):
        kept = jnp.where(first, value[:half], value[3 * half:])
        crossed = jnp.where(first, value[half:2 * half], value[2 * half:3 * half])
        return kept + pltpu.roll(crossed, rank, 1)

    def stack(at, value):
        top, low = split(value)
        stacked[0:half, at] = top
        stacked[half:2 * half, at] = low
        stacked[2 * half:3 * half, at] = top

    group = 8
    for base in range(0, rows, group):
        for n in range(base, base + group):
            stack(slice(n * lane, (n + 1) * lane), turned[pl.ds(n, half, stride=rows), :])
    for base in range(0, rows, group):
        span = slice(base * lane, (base + group) * lane)
        value = product(lhs_forward, stacked[:, span])
        for n in range(group):
            scaled = gather_halves(value[:, n * lane:(n + 1) * lane]) * inverse
            stack(slice((base + n) * lane, (base + n + 1) * lane), scaled)
    for base in range(0, rows, group):
        span = slice(base * lane, (base + group) * lane)
        value = product(lhs_back, stacked[:, span])
        for n in range(group):
            turned[pl.ds(base + n, half, stride=rows), :] = gather_halves(value[:, n * lane:(n + 1) * lane])
    return jnp.concatenate([a_top, a_top, a_low], axis=1)


def condition_chunk(turned, c, rows, per_chunk, a_all, write):
    lane = turned.shape[1]
    top, low = split(turned[pl.ds(pl.multiple_of(c * per_chunk * rows, 8), per_chunk * rows), :])
    value = product(jnp.concatenate([top, low, top], axis=1), a_all, across).astype(jnp.bfloat16)
    for i in range(per_chunk):
        write(slice(i * lane, (i + 1) * lane), value[i * rows:(i + 1) * rows])

def nth_block(j, zz, line):
    lefts = zz
    rights = line - 1 - zz
    both_ways = jnp.minimum(lefts, rights)
    i = j - 1
    paired = i < 2 * both_ways
    t = jnp.where(paired, i // 2 + 1, j - both_ways)
    from_left = jnp.where(paired, jnp.asarray(i % 2 == 0).astype(jnp.int32), (lefts > rights).astype(jnp.int32))
    return jnp.where(from_left > 0, zz - t, zz + t)


def score_kernel(
    line, queries_ref, s_ref, a_ref, eig_ref, ids_ref, train_ref, total, acc, arrived, hot,
    turned, stacked, stored, turned_train, held,
    load_sem, z_recv, y_recv, x_recv, z_send, y_send, x_send, c_send, c_recv,
):
    grp = lax.axis_index("grp")
    ex = lax.axis_index("ex")
    core = lax.axis_index("lay")
    zz = ex // 2
    w = ex % 2
    side = grp % 2
    rows = queries_ref.shape[0]
    examples = train_ref.shape[0]
    chunk = queries_ref.shape[1] // chunks
    half = examples // 2
    window = examples // slices
    right = {"ex": lax.rem(ex + 2, 2 * line)}
    left = {"ex": lax.rem(ex + 2 * line - 2, 2 * line)}
    across_y = {"ex": zz * 2 + (1 - w)}
    across_x = {"grp": (grp // 2) * 2 + (1 - side)}
    across_c = {"lay": 1 - core}
    has_left = zz > 0
    has_right = zz < line - 1
    both_ways = jnp.minimum(zz, line - 1 - zz)

    def z_chunk(k):
        return jnp.where(
            k < 2, 2 * side + k, jnp.where(
                k == 2, 4 + side, jnp.where(k < 5, 3 + k, jnp.where(k == 5, 5 - side, 3 - 2 * side))
            )
        )

    def own_chunk(k):
        return jnp.where(k < 2, 2 * side + k, jnp.where(k == 2, 4 + side, 6 + side))

    def remote(src, dst, send, recv, target):
        return pltpu.make_async_remote_copy(
            src_ref=src, dst_ref=dst, send_sem=send, recv_sem=recv,
            device_id=target, device_id_type=MESH,
        )

    def load(c):
        return pltpu.make_async_copy(
            train_ref.at[:, pl.ds(c * chunk, chunk)], stored.at[c], load_sem
        )

    def z_copy(b, k, target):
        slot = held.at[b, z_chunk(k), w]
        return remote(slot, slot, z_send, z_recv.at[b, k], target)

    def y_copy(b, k, c, column):
        slot = held.at[b, c, column]
        return remote(slot, slot, y_send, y_recv.at[b, k], across_y)

    def x_copy(b, k, c, column):
        slot = held.at[b, c, column]
        return remote(slot, slot, x_send, x_recv.at[b, k], across_x)

    def c_copy(b):
        return remote(acc.at[b], arrived.at[b], c_send, c_recv.at[b], across_c)

    def block_of(j):
        return nth_block(j, zz, line)

    @pl.loop(0, chunks)
    def _(c):
        load(c).start()

    barrier = pltpu.get_barrier_semaphore()

    @pl.when(has_left)
    def _():
        pl.semaphore_signal(barrier, inc=1, device_id=left, device_id_type=MESH)

    @pl.when(has_right)
    def _():
        pl.semaphore_signal(barrier, inc=1, device_id=right, device_id_type=MESH)

    for target in (across_y, across_x, across_c):
        pl.semaphore_signal(barrier, inc=1, device_id=target, device_id_type=MESH)

    a_all = rotate(queries_ref, s_ref, a_ref, eig_ref, turned, stacked)

    def condition(c):
        def write(at, value):
            held[zz, c, w, :, at] = value

        condition_chunk(turned, c, rows, chunk // turned.shape[1], a_all, write)

    pl.semaphore_wait(barrier, 3 + has_left.astype(jnp.int32) + has_right.astype(jnp.int32))

    def send_z(k):
        @pl.when(has_right)
        def _():
            z_copy(zz, k, right).start()

        @pl.when(has_left)
        def _():
            z_copy(zz, k, left).start()

    @pl.loop(0, 6)
    def _(k):
        condition(z_chunk(k))
        send_z(k)

        @pl.when(k < 3)
        def _():
            y_copy(zz, k, own_chunk(k), w).start()

        @pl.when(k == 4)
        def _():
            y_copy(zz, 3, own_chunk(3), w).start()

    @pl.loop(0, 2)
    def _(k):
        condition(2 - 2 * side + k)

    ids = ids_ref[...].astype(jnp.float32)
    wanted = jnp.where(core == 0, ids[:, :half], ids[:, half:])
    for tile in range(examples // 128):
        row = lax.broadcasted_iota(jnp.int32, (128, half), 0).astype(jnp.float32) + float(tile * 128)
        hot[tile * 128:(tile + 1) * 128, :] = jnp.where(row == wanted, 1.0, 0.0).astype(jnp.bfloat16)

    def z_arrival(b, k, from_left, near):
        z_copy(b, k, right).wait_recv()
        if from_left:
            @pl.when(has_right)
            def _():
                z_copy(b, k, right).start()
        else:
            @pl.when(has_left)
            def _():
                z_copy(b, k, left).start()

        @pl.when(k < 5)
        def _():
            y_copy(b, k, z_chunk(k), w).start()

        @pl.when(jnp.logical_or(k == 0, jnp.logical_and(k == 1, jnp.logical_not(near))))
        def _():
            x_copy(b, k, z_chunk(k), w).start()

    def y_arrival(r):
        shared = r < 10 * both_ways
        t = r // 10 + 1
        near = jnp.where(r % 2 == 0, zz - t, zz + t)
        b = jnp.where(shared, near, block_of(r // 5 + 1))
        k = jnp.where(shared, r % 10 // 2, r % 5)
        y_copy(b, k, z_chunk(k), 1 - w).wait_recv()

        @pl.when(k < 3)
        def _():
            x_copy(b, k + 2, z_chunk(k), 1 - w).start()

    def relay(tick):
        t = tick // 6 + 1
        k = tick % 6

        @pl.when(jnp.logical_and(t < line, zz - t >= 0))
        def _():
            z_arrival(zz - t, k, True, t == 1)

        @pl.when(jnp.logical_and(t < line, zz + t < line))
        def _():
            z_arrival(zz + t, k, False, t == 1)

        @pl.when(jnp.asarray(tick) == late)
        def _():
            send_z(6)

        q = tick

        @pl.when(q < 4)
        def _():
            y_copy(zz, q, own_chunk(q), 1 - w).wait_recv()
            x_copy(zz, q, own_chunk(q), 1 - w).start()

        @pl.when(jnp.logical_and(q >= 4, q < 5 * line - 2))
        def _():
            y_arrival(q - 4)

    def turn_train(c):
        eye = picks((edge, edge), lambda r, c: r == c)
        for at in range(0, chunk, edge):
            for n in range(slices):
                columns = slice(n * window, (n + 1) * window)
                turned_train[c, at:at + edge, columns] = product(
                    eye, stored[c, columns, at:at + edge], across
                ).astype(jnp.bfloat16)

    def put(blocks, n, picked, more=False):
        columns = slice(n * window, (n + 1) * window)
        value = None
        for c in picked:
            queries = [held[b, c].reshape(2 * rows, chunk) for b in blocks]
            term = product(jnp.concatenate(queries, axis=0), turned_train[c, :, columns])
            value = term if value is None else value + term
        for i, b in enumerate(blocks):
            part = value[i * 2 * rows:(i + 1) * 2 * rows]
            acc[b, :, columns] = acc[b, :, columns] + part if more else part

    def put_all(blocks, picked, more=False):
        for n in range(slices):
            put(blocks, n, picked, more)

    def last_arrivals(b):
        x_copy(b, 0, 0, w).wait_recv()
        for k in (2, 3):
            x_copy(b, k, 0, w).wait_recv()
        near = jnp.abs(b - zz) == 1

        @pl.when(near)
        def _():
            z_copy(b, 6, right).wait_recv()

        @pl.when(jnp.logical_not(near))
        def _():
            x_copy(b, 1, 0, w).wait_recv()

        @pl.when(b != zz)
        def _():
            x_copy(b, 4, 0, w).wait_recv()

    def finish(blocks):
        for b in blocks:
            c_copy(b).wait_recv()
        both = jnp.concatenate([acc[b] + arrived[b] for b in blocks], axis=0)
        value = product(jnp.concatenate(split(both), axis=0), hot[...])
        value = value[:both.shape[0]] + value[both.shape[0]:]
        for i, b in enumerate(blocks):
            total[b] = value[i * 2 * rows:(i + 1) * 2 * rows]

    mine = (2 * side, 2 * side + 1, 4 + side, 6, 7)
    pair = (2 - 2 * side, 3 - 2 * side)
    single = (5 - side,)
    last = block_of(line - 1)
    ticks = max(6 * (line - 1), 5 * line - 2)

    def compute(tick):
        @pl.when(tick < chunks)
        def _():
            @pl.when(tick == 0)
            def _():
                pltpu.make_async_copy(stored, stored, load_sem).wait()

            turn_train(tick)

        for n in range(slices):
            @pl.when(tick == own_tick + n)
            def _():
                if n == 0:
                    for k in range(4):
                        x_copy(zz, k, 0, w).wait_recv()

                put([zz], n, range(chunks))

                if n == slices - 1:
                    c_copy(zz).start()

        @pl.when(tick == own_tick + 6)
        def _():
            finish([zz])

        p = (tick - 1) // 12
        step = (tick - 1) % 12
        one = block_of(2 * p - 1)
        other = block_of(2 * p)
        inside = jnp.logical_and(p >= 1, p < line // 2)

        for n in range(slices):
            @pl.when(jnp.logical_and(inside, step == n))
            def _():
                put([one, other], n, mine)

        @pl.when(jnp.logical_and(inside, step == 3))
        def _():
            last_arrivals(one)
            last_arrivals(other)

            put_all([one, other], pair + single, True)

            c_copy(one).start()
            c_copy(other).start()

        @pl.when(jnp.logical_and(inside, jnp.logical_and(step == 9, p < line // 2 - 1)))
        def _():
            finish([one, other])

    @pl.loop(0, ticks)
    def _(tick):
        relay(tick)
        compute(tick)

    put_all([last], mine[:4])

    y_arrival(5 * line - 6)

    for k in range(4):
        x_copy(last, k, 0, w).wait_recv()

    put_all([last], mine[4:] + pair, True)

    x_copy(last, 4, 0, w).wait_recv()

    def c_part(b, n):
        columns = slice(n * window, (n + 1) * window)
        return remote(acc.at[b, :, columns], arrived.at[b, :, columns], c_send, c_recv.at[b], across_c)

    for n in range(slices):
        put([last], n, single, True)
        c_part(last, n).start()

    finish([block_of(line - 3), block_of(line - 2)])
    def sent(count, send):
        span = train_ref.at[pl.ds(0, count * rows // 2), pl.ds(0, 2 * chunk)]
        remote(span, span, send, c_recv.at[0], across_c).wait_send()

    at_end = both_ways == 0

    @pl.when(at_end)
    def _():
        sent(7, z_send)
        sent(5 * line - 2, x_send)

    @pl.when(jnp.logical_not(at_end))
    def _():
        sent(6 * line + 8, z_send)
        sent(5 * line - 3, x_send)

    sent(5 * line - 1, y_send)
    remote(acc, arrived, c_send, c_recv.at[0], across_c).wait_send()
    c_copy(last).wait_recv()


def scores_of(queries, basis_s, basis_a, eigvals, ids, train, devices):
    rows = queries.shape[0]
    chunk = queries.shape[1] // chunks
    rank = basis_s.shape[0]
    examples = train.shape[0]
    line = devices // 2
    dma = pltpu.SemaphoreType.DMA
    vmem = pl.BlockSpec(memory_space=pltpu.VMEM)
    return pl.pallas_call(
        functools.partial(score_kernel, line),
        out_shape=[
            pltpu.VMEM((line, 2 * rows, examples // 2), jnp.float32),
            pltpu.VMEM((line, 2 * rows, examples), jnp.float32),
            pltpu.VMEM((line, 2 * rows, examples), jnp.float32),
            pltpu.VMEM((examples, examples // 2), jnp.bfloat16),
        ],
        in_specs=[vmem] * 5 + [pl.BlockSpec(memory_space=pltpu.HBM)],
        out_specs=[vmem] * 4,
        scratch_shapes=[
            pltpu.VMEM((rank // 2 * rows, 2 * rank), jnp.float32),
            pltpu.VMEM((3 * rank // 2, rows * 2 * rank), jnp.bfloat16),
            pltpu.VMEM((chunks, examples, chunk), jnp.bfloat16),
            pltpu.VMEM((chunks, chunk, examples), jnp.bfloat16),
            pltpu.VMEM((line, chunks, 2, rows, chunk), jnp.bfloat16),
            dma,
            dma((line, 7)),
            dma((line, 5)),
            dma((line, 5)),
            *[dma] * 4,
            dma((line,)),
        ],
        compiler_params=pltpu.CompilerParams(
            collective_id=0, has_side_effects=True, vmem_limit_bytes=52 * 1024 * 1024
        ),
    )(queries, basis_s, basis_a, eigvals, ids, train)


def finish_kernel(line, total_ref, acc_ref, arrived_ref, hot_ref, out_ref, done, sems):
    zz = lax.axis_index("ex") // 2
    rows = total_ref.shape[1]
    last = nth_block(line - 1, zz, line)

    def out_copy(b, source):
        return pltpu.make_async_copy(source, out_ref.at[b], sems.at[b])

    @pl.loop(0, line)
    def _(b):
        @pl.when(b != last)
        def _():
            out_copy(b, total_ref.at[b]).start()

    value = product(jnp.concatenate(split(acc_ref[last] + arrived_ref[last]), axis=0), hot_ref[...])
    done[...] = value[:rows] + value[rows:]
    out_copy(last, done).start()

    @pl.loop(0, line)
    def _(b):
        out_copy(b, done).wait()


def finished(total, acc, arrived, hot):
    line = total.shape[0]
    vmem = pl.BlockSpec(memory_space=pltpu.VMEM)
    return pl.pallas_call(
        functools.partial(finish_kernel, line),
        out_shape=jax.ShapeDtypeStruct(total.shape, jnp.float32),
        in_specs=[vmem] * 4,
        out_specs=pl.BlockSpec(memory_space=pl.ANY),
        scratch_shapes=[
            pltpu.VMEM(total.shape[1:], jnp.float32),
            pltpu.SemaphoreType.DMA((line,)),
        ],
        compiler_params=pltpu.CompilerParams(vmem_limit_bytes=8 * 1024 * 1024),
    )(total, acc, arrived, hot)


def shards(devices, queries, basis_s, basis_a, eigvals, train_grads, example_ids):
    parts = scores_of(
        queries.reshape(queries.shape[0], -1), basis_s[0], basis_a[0], eigvals[0],
        example_ids, train_grads.reshape(train_grads.shape[0], -1), devices,
    )
    return finished(*parts).reshape(devices * queries.shape[0], -1)


def solution(mesh):
    return jax.shard_map(
        functools.partial(shards, mesh.shape["ex"]),
        mesh=mesh,
        in_specs=(
            P("ex", "lay", None),
            P("lay", None, None),
            P("lay", None, None),
            P("lay", None, None),
            P(("grp", "ex"), "lay", None),
            P(("grp", "ex"), None),
        ),
        out_specs=P(None, ("grp", "ex", "lay")),
        check_vma=False,
    )
```
